256 devices in a mesh: roll: 8 (over z), fsdp: 32 (over y, x, core).
Axes of the slice: x: 4, y: 4, z: 8, core: 2. Of those that a mesh axis runs over, the one named last changes fastest.
Arguments:
- hidden: bfloat16 [32768, 4096], P(('roll', 'fsdp')), may hold values from -24 to 24
- send_counts: int32 [32, 8, 8], P('fsdp'), may hold values from 8 to 24, as said below
- queries: bfloat16 [32768, 4096], P(('roll', 'fsdp')), may hold values from -90 to 90
- upstream: bfloat16 [32768, 4096], P(('roll', 'fsdp')), may hold values from -6 to 6
- norm_gain: float32 [4096], replicated, may hold values from 0.5 to 1.5
- kv_weight: bfloat16 [4096, 1024], P('fsdp'), may hold values from -0.09375 to 0.09375
- logp_new: float32 [256, 128], P(('roll', 'fsdp')), may hold values from -3 to 0
- logp_old: float32 [256, 128], P(('roll', 'fsdp')), may hold values from -3 to 0
- advantage: float32 [256, 4], P(('roll', 'fsdp')), may hold values from -4 to 4
- segment_ids: int32 [256, 128], P(('roll', 'fsdp')), may hold values from 0 to 3, never falling along the last dimension, each value on 1 to 64 neighbouring positions
- trim_mask: int32 [256, 128], P(('roll', 'fsdp')), may hold values 0 or 1
Outputs:
- d_queries: bfloat16 [32768, 4096], P(('roll', 'fsdp'))
- d_hidden: bfloat16 [32768, 4096], P(('roll', 'fsdp'))
- kv_grad: float32 [4096, 1024], P('fsdp')
The draws below stay inside these ranges and needn't reach their ends.
Inputs may be any that keep to these rules, and one draw needn't show every extreme that they name: For each fsdp index, every row and every column of send_counts sums to 128; a rollout shard's rows are ordered by the learner shard they go to.
All inputs are finite; a program needn't handle non-finite values. No bound on the sum of `trim_mask` on one device may be relied on, other than what follows from the above.
Results may differ from the reference program's by a relative error of at most 0.008.
The reference program's roundings to bfloat16 on the way count: a program that leaves them out, or rounds other values in their place, can miss the bound.
Values may be sent and summed in bfloat16 or wider, within the bound.
A program may use at most 128 MiB of HBM per device.

```python
import math
import jax
import jax.numpy as jnp
import numpy as np
from jax import lax

D = 4096
KV = 4
HD = 128
GROUP = 8
TOK_DEV = 128
RESP_DEV = 4
LEARNERS = 8
GROUPS = 32
BLOCKS = 256
TOKENS = 32768
KVW = 512
QW = 4096


def draw_send_counts(key, part):

    def one_group(group_key):
        base_rows = TOK_DEV // LEARNERS
        half_rows = base_rows // 2
        key_values, key_order = jax.random.split(group_key)
        offsets = jax.random.randint(key_values, (LEARNERS // 2,), 0, half_rows + 1)
        offsets = offsets.at[0].set(half_rows)
        pattern = jnp.concatenate([offsets, -offsets])
        shuffled = pattern[jax.random.permutation(key_order, LEARNERS)]
        source = jnp.arange(LEARNERS)[:, None]
        target = jnp.arange(LEARNERS)[None, :]
        return (base_rows + shuffled[(target - source) % LEARNERS]).astype(jnp.int32)
    return jax.vmap(one_group)(jax.random.split(key, GROUPS))


def draw_queries(key, part):
    key_base, key_scale = jax.random.split(key, 2)
    base_draw = jax.random.normal(key_base, (TOKENS, QW), jnp.float32)
    row_scale = jnp.exp(jax.random.uniform(key_scale, (TOKENS, 1), jnp.float32, math.log(0.5), math.log(5.0)))
    return jnp.clip(base_draw * row_scale, -90.0, 90.0).astype(jnp.bfloat16)


def touch_ends(array, own_key, smallest, largest):
    place = [jax.random.randint(jax.random.fold_in(own_key, axis), (), 0, length) for axis, length in enumerate(array.shape)]
    longest = array.shape.index(max(array.shape))
    next_to = place[:longest] + [(place[longest] + 1) % array.shape[longest]] + place[longest + 1:]
    return array.at[tuple(place)].set(smallest).at[tuple(next_to)].set(largest)


def with_spikes(drawn, rng, source, target, shards_of, factor):
    def block_of(dim):
        return (jnp.arange(drawn.shape[dim]) // (drawn.shape[dim] // shards_of)).reshape((-1,) + (1,) * (drawn.ndim - 1 - dim))

    one_side = jax.random.permutation(rng, shards_of)[block_of(target)]
    far = (block_of(target) + shards_of // 2) % shards_of
    return jnp.where((block_of(source) == one_side) | (block_of(source) == far), factor * drawn, drawn)


def level_of(stream_key, extent, cuts, low, high):
    loudness, own = 1.0, jax.random.fold_in(stream_key, 6)
    for dim, parts in cuts:
        steps = jnp.exp(jax.random.uniform(jax.random.fold_in(own, dim), (parts,), jnp.float32, low / len(cuts), high / len(cuts)))
        loudness = loudness * jnp.repeat(steps, extent[dim] // parts).reshape([-1 if axis == dim else 1 for axis in range(len(extent))])
    return loudness


def split_up(number_of, total, limit, skew):
    portions = [(1 << 20) // math.isqrt(grade ** skew) + 1 for grade in range(2, number_of + 1)]
    rest, given = total - limit - (number_of - 1), [1] * (number_of - 1)
    while rest > 0:
        free = [i for i in range(number_of - 1) if given[i] < limit]
        pool, left = sum([portions[i] for i in free]), rest
        for i in free:
            extra = min(limit - given[i], max(1, left * portions[i] // pool), rest)
            given[i] = given[i] + extra
            rest = rest - extra
    return np.array([limit] + given)


def uneven(own_key, amount, total, bound, skew):
    if amount == 2:
        one = jax.random.randint(own_key, (), max(1, total - bound), min(bound, total - 1) + 1)
        return jnp.stack([one, total - one])
    tallies = jnp.asarray(split_up(amount, total, bound, skew), jnp.int32)
    couples = (amount - 1) // 2
    donor, sink = tallies[1:1 + 2 * couples:2], tallies[2:2 + 2 * couples:2]
    slack = jnp.minimum(donor - 1, bound - sink)
    shifted = jax.random.randint(jax.random.fold_in(own_key, 1), (couples,), 0, 1 << 20) % (slack + 1)
    tallies = tallies.at[1:1 + 2 * couples:2].set(donor - shifted).at[2:2 + 2 * couples:2].set(sink + shifted)
    return tallies[jax.random.permutation(jax.random.fold_in(own_key, 2), amount)]


def bell_draw(own_key, extent, scale, most, cuts=(), held_as=jnp.bfloat16):
    loudness = level_of(own_key, extent, cuts, -0.22, 0.18) if cuts else 1.0
    result = jax.random.normal(own_key, extent, jnp.float32) * scale * loudness
    return jnp.minimum(jnp.maximum(result, -most), most).astype(held_as)


def heavy_noise(key, extent, spread, limit, cuts, heavy, kind=jnp.bfloat16):
    entries = spread * jax.random.normal(key, extent, jnp.float32)
    if cuts:
        entries = entries * level_of(key, extent, cuts, -0.22, 0.18)
    return jnp.clip(with_spikes(entries, jax.random.fold_in(key, 3), *heavy), -limit, limit).astype(kind)


def setup_inputs(seed: int = 0) -> dict:
    seeds = jax.random.split(jax.random.key(seed), 12)
    hidden = heavy_noise(seeds[0], (TOKENS, D), 1.0, 24.0, ((0, 256),), (0, 1, 256, 6.0))
    send_counts = draw_send_counts(jax.random.fold_in(seeds[11], 71), 0)
    queries = draw_queries(jax.random.fold_in(seeds[11], 71), 0)
    upstream = bell_draw(seeds[3], (TOKENS, QW), 1.0, 6.0, ((0, 256),))
    norm_gain = jnp.clip(1.0 + 0.1 * jax.random.normal(seeds[4], (D,), jnp.float32), 0.5, 1.5)
    kv_weight = bell_draw(seeds[5], (D, 2 * KVW), D ** -0.5, 0.09375, ((0, 32),))
    logp_new = jnp.clip(-3.0 + 3.0 * jax.random.uniform(seeds[6], (BLOCKS, TOK_DEV), jnp.float32) ** level_of(seeds[6], (BLOCKS, TOK_DEV), ((0, 256),), -0.2, 0.2), -3.0, 0.0)
    logp_old = jnp.clip(-3.0 + 3.0 * jax.random.uniform(seeds[7], (BLOCKS, TOK_DEV), jnp.float32) ** level_of(seeds[7], (BLOCKS, TOK_DEV), ((0, 256),), -0.2, 0.2), -3.0, 0.0)
    advantage = bell_draw(seeds[8], (BLOCKS, RESP_DEV), 1.0, 4.0, ((0, 256),), jnp.float32)
    segment_ids = jax.vmap(lambda own: jnp.searchsorted(jnp.cumsum(uneven(own, RESP_DEV, TOK_DEV, TOK_DEV // 2, 2)), jnp.arange(TOK_DEV), side="right"))(jax.random.split(seeds[9], BLOCKS)).reshape((BLOCKS, TOK_DEV)).astype(jnp.int32)
    trim_mask = touch_ends((jax.random.randint(seeds[10], (BLOCKS, TOK_DEV), 0, 8) < 7).astype(jnp.int32), jax.random.fold_in(seeds[10], 1), 0, 1)
    return {"hidden": hidden, "send_counts": send_counts, "queries": queries, "upstream": upstream, "norm_gain": norm_gain, "kv_weight": kv_weight, "logp_new": logp_new, "logp_old": logp_old, "advantage": advantage, "segment_ids": segment_ids, "trim_mask": trim_mask}


ratio_cap = 2.0
norm_eps = 1e-06

def relay_order(send_counts):
    send_starts = jnp.cumsum(send_counts, axis=2) - send_counts
    recv_starts = jnp.cumsum(send_counts, axis=1) - send_counts
    recv_learner = jnp.transpose(recv_starts, (0, 2, 1))
    send_learner = jnp.transpose(send_starts, (0, 2, 1))
    position = jnp.arange(TOK_DEV, dtype=jnp.int32)
    owner_shard = lax.optimization_barrier(jnp.sum((position[None, None, :, None] >= recv_learner[:, :, None, :]).astype(jnp.int32), axis=3)) - 1
    matches = owner_shard[:, :, :, None] == jnp.arange(LEARNERS, dtype=jnp.int32)[None, None, None, :]
    begin_recv = lax.optimization_barrier(jnp.sum(jnp.where(matches, recv_learner[:, :, None, :], 0), axis=3))
    begin_send = lax.optimization_barrier(jnp.sum(jnp.where(matches, send_learner[:, :, None, :], 0), axis=3))
    group_index = jnp.arange(GROUPS, dtype=jnp.int32)[:, None, None]
    source_row = (owner_shard * GROUPS + group_index) * TOK_DEV + begin_send + position[None, None, :] - begin_recv
    return jnp.transpose(source_row, (1, 0, 2)).reshape(-1).astype(jnp.int32)

def token_weight(logp_new, logp_old, advantage, segment_ids, trim_mask):
    clipped = jnp.minimum(jnp.exp(logp_new - logp_old), ratio_cap)
    response = jnp.arange(advantage.shape[1], dtype=jnp.int32)
    picked = lax.optimization_barrier(jnp.sum(jnp.where(segment_ids[:, :, None] == response[None, None, :], advantage[:, None, :], 0.0), axis=2))
    return trim_mask.astype(jnp.float32) * picked * clipped

def block_backward(query_rows, kv_rows, upstream_rows, weight_rows, segment_rows):
    tok_rows = query_rows.shape[0]
    kv_width = KV * HD
    keys_block = kv_rows[:, :kv_width].reshape(tok_rows, KV, HD).astype(jnp.float32)
    values_block = kv_rows[:, kv_width:].reshape(tok_rows, KV, HD).astype(jnp.float32)
    query_heads = query_rows.reshape(tok_rows, KV, GROUP, HD)
    score_scale = 1.0 / math.sqrt(HD)
    scores = jnp.einsum('ikgd,jkd->kgij', query_heads.astype(jnp.float32), keys_block) * score_scale
    position = jnp.arange(tok_rows, dtype=jnp.int32)
    allowed = (segment_rows[:, None] == segment_rows[None, :]) & (position[None, :] <= position[:, None])
    scores = jnp.where(allowed[None, None], scores, -jnp.inf)
    row_max = lax.optimization_barrier(jnp.max(scores, axis=3, keepdims=True))
    expo = jnp.exp(scores - row_max)
    probs = expo / lax.optimization_barrier(jnp.sum(expo, axis=3, keepdims=True))
    probs_low = probs.astype(jnp.bfloat16)
    attended = jnp.einsum('kgij,jkd->ikgd', probs_low.astype(jnp.float32), values_block)
    d_out = (weight_rows[:, None] * upstream_rows.astype(jnp.float32)).astype(jnp.bfloat16)
    d_out = d_out.reshape(tok_rows, KV, GROUP, HD).astype(jnp.float32)
    row_delta = lax.optimization_barrier(jnp.sum(d_out * attended, axis=3))
    d_probs = jnp.einsum('ikgd,jkd->kgij', d_out, values_block)
    d_scores = (probs * (d_probs - jnp.transpose(row_delta, (1, 2, 0))[..., None]) * score_scale).astype(jnp.bfloat16)
    d_scores = d_scores.astype(jnp.float32)
    d_query = jnp.einsum('kgij,jkd->ikgd', d_scores, keys_block).astype(jnp.bfloat16).reshape(tok_rows, -1)
    d_keys = jnp.einsum('kgij,ikgd->jkd', d_scores, query_heads.astype(jnp.float32))
    d_values = jnp.einsum('kgij,ikgd->jkd', probs_low.astype(jnp.float32), d_out)
    d_kv = jnp.concatenate([d_keys.reshape(tok_rows, kv_width), d_values.reshape(tok_rows, kv_width)], axis=1)
    return (d_query, d_kv.astype(jnp.bfloat16))

def reference(hidden, send_counts, queries, upstream, norm_gain, kv_weight, logp_new, logp_old, advantage, segment_ids, trim_mask):
    order = relay_order(send_counts)
    relaid = jnp.take(hidden, order, axis=0)
    values_f = relaid.astype(jnp.float32)
    inv_rms = lax.rsqrt(lax.optimization_barrier(jnp.mean(values_f * values_f, axis=1, keepdims=True)) + norm_eps)
    unit_rows = values_f * inv_rms
    normed = (unit_rows * norm_gain).astype(jnp.bfloat16)
    keys_values = jnp.dot(normed, kv_weight, preferred_element_type=jnp.float32).astype(jnp.bfloat16)
    coefficient = token_weight(logp_new, logp_old, advantage, segment_ids, trim_mask)
    packed = (queries.reshape(BLOCKS, TOK_DEV, QW), keys_values.reshape(BLOCKS, TOK_DEV, 2 * KVW), upstream.reshape(BLOCKS, TOK_DEV, QW), coefficient, segment_ids)
    d_query, d_kv = lax.map(lambda items: block_backward(*items), packed)
    d_queries = d_query.reshape(TOKENS, QW)
    d_kv = d_kv.reshape(TOKENS, 2 * KVW)
    kv_grad = lax.dot_general(normed, d_kv, (((0,), (0,)), ((), ())), preferred_element_type=jnp.float32)
    kv_grad = kv_grad * (1.0 / math.sqrt(TOKENS))
    d_normed = lax.dot_general(d_kv, kv_weight, (((1,), (1,)), ((), ())), preferred_element_type=jnp.float32)
    d_unit = d_normed * norm_gain
    d_relaid = (inv_rms * (d_unit - unit_rows * lax.optimization_barrier(jnp.mean(d_unit * unit_rows, axis=1, keepdims=True)))).astype(jnp.bfloat16)
    d_hidden = jnp.zeros_like(hidden).at[order].set(d_relaid)
    return (d_queries, d_hidden, kv_grad)
```

```python
import math

import jax
import jax.numpy as jnp
from jax import lax
from jax.sharding import PartitionSpec as P

KV = 4
HD = 128
GROUP = 8


ratio_cap = 2.0
norm_eps = 1e-06


def exclusive_starts(counts):
    return jnp.cumsum(counts) - counts


def pack_rows(source_rows, starts, slot_cap):
    slot_index = jnp.arange(slot_cap, dtype=jnp.int32)
    picks = jnp.minimum(starts[:, None] + slot_index[None, :], source_rows.shape[0] - 1)
    chosen = jnp.take(source_rows, picks.reshape(-1), axis=0)
    return chosen.reshape(starts.shape[0], slot_cap, source_rows.shape[1])


def unpack_rows(buffer, starts, tok_rows):
    peer_count, slot_cap, row_width = buffer.shape
    position = jnp.arange(tok_rows, dtype=jnp.int32)
    owner_shard = jnp.sum((position[:, None] >= starts[None, :]).astype(jnp.int32), axis=1) - 1
    slot_index = position - jnp.take(starts, owner_shard)
    flat_index = owner_shard * slot_cap + slot_index
    return jnp.take(buffer.reshape(peer_count * slot_cap, row_width), flat_index, axis=0)


def token_weight(logp_new, logp_old, advantage, segment_ids, trim_mask):
    clipped = jnp.minimum(jnp.exp(logp_new - logp_old), ratio_cap)
    response = jnp.arange(advantage.shape[1], dtype=jnp.int32)
    picked = jnp.sum(
        jnp.where(segment_ids[:, :, None] == response[None, None, :], advantage[:, None, :], 0.0),
        axis=2,
    )
    return trim_mask.astype(jnp.float32) * picked * clipped


def normalize(source_rows, norm_gain):
    values_f = source_rows.astype(jnp.float32)
    inv_rms = lax.rsqrt(jnp.mean(values_f * values_f, axis=1, keepdims=True) + norm_eps)
    unit_rows = values_f * inv_rms
    return ((unit_rows * norm_gain).astype(jnp.bfloat16), unit_rows, inv_rms)


def attend(queries, keys_values, upstream, coefficient, segment_rows):
    tok_rows = queries.shape[0]
    kv_width = KV * HD
    keys_block = keys_values[:, :kv_width].reshape(tok_rows, KV, HD)
    values_block = keys_values[:, kv_width:].reshape(tok_rows, KV, HD)
    query_heads = queries.reshape(tok_rows, KV, GROUP, HD)
    score_scale = 1.0 / math.sqrt(HD)
    scores = (
        jnp.einsum("ikgd,jkd->kgij", query_heads, keys_block, preferred_element_type=jnp.float32)
        * score_scale
    )
    position = jnp.arange(tok_rows, dtype=jnp.int32)
    allowed = (segment_rows[:, None] == segment_rows[None, :]) & (
        position[None, :] <= position[:, None]
    )
    scores = jnp.where(allowed[None, None], scores, -jnp.inf)
    row_max = jnp.max(scores, axis=3, keepdims=True)
    expo = jnp.exp(scores - row_max)
    probs = expo / jnp.sum(expo, axis=3, keepdims=True)
    probs_low = probs.astype(jnp.bfloat16)
    attended = jnp.einsum(
        "kgij,jkd->ikgd", probs_low, values_block, preferred_element_type=jnp.float32
    )
    d_out = (coefficient[:, None] * upstream.astype(jnp.float32)).astype(jnp.bfloat16)
    d_out = d_out.reshape(tok_rows, KV, GROUP, HD)
    row_delta = jnp.sum(d_out.astype(jnp.float32) * attended, axis=3)
    d_probs = jnp.einsum("ikgd,jkd->kgij", d_out, values_block, preferred_element_type=jnp.float32)
    d_scores = (
        probs * (d_probs - jnp.transpose(row_delta, (1, 2, 0))[..., None]) * score_scale
    ).astype(jnp.bfloat16)
    d_query = jnp.einsum("kgij,jkd->ikgd", d_scores, keys_block, preferred_element_type=jnp.float32)
    d_query = d_query.astype(jnp.bfloat16).reshape(tok_rows, -1)
    d_keys = jnp.einsum("kgij,ikgd->jkd", d_scores, query_heads, preferred_element_type=jnp.float32)
    d_values = jnp.einsum("kgij,ikgd->jkd", probs_low, d_out, preferred_element_type=jnp.float32)
    d_kv = jnp.concatenate(
        [d_keys.reshape(tok_rows, kv_width), d_values.reshape(tok_rows, kv_width)], axis=1
    )
    return (d_query, d_kv.astype(jnp.bfloat16))


def shards(
    hidden,
    send_counts,
    queries,
    upstream,
    norm_gain,
    kv_weight,
    logp_new,
    logp_old,
    advantage,
    segment_ids,
    trim_mask,
):
    tok_rows = hidden.shape[0]
    roll_size = lax.axis_size("roll")
    fsdp_size = lax.axis_size("fsdp")
    slot_cap = tok_rows // roll_size + tok_rows // (2 * roll_size)
    my_roll = lax.axis_index("roll")
    group_counts = send_counts[0]
    send_starts = exclusive_starts(jnp.take(group_counts, my_roll, axis=0))
    recv_starts = exclusive_starts(jnp.take(group_counts, my_roll, axis=1))
    full_weight = lax.all_gather(kv_weight, "fsdp", axis=0, tiled=True)
    coefficient = token_weight(logp_new, logp_old, advantage, segment_ids, trim_mask)[0]
    normed, unit_rows, inv_rms = normalize(hidden, norm_gain)
    normed_columns = lax.all_to_all(
        normed.reshape(tok_rows, fsdp_size, -1), "fsdp", split_axis=1, concat_axis=0, tiled=True
    ).reshape(tok_rows * fsdp_size, -1)
    projected = jnp.dot(normed, full_weight, preferred_element_type=jnp.float32).astype(
        jnp.bfloat16
    )
    arrived = lax.all_to_all(
        pack_rows(projected, send_starts, slot_cap), "roll", split_axis=0, concat_axis=0, tiled=True
    )
    keys_values = unpack_rows(arrived, recv_starts, tok_rows)
    d_queries, d_kv = attend(queries, keys_values, upstream, coefficient, segment_ids[0])
    returned = lax.all_to_all(
        pack_rows(d_kv, recv_starts, slot_cap), "roll", split_axis=0, concat_axis=0, tiled=True
    )
    d_projected = unpack_rows(returned, send_starts, tok_rows)
    plane_d = lax.all_gather(d_projected, "fsdp", axis=0, tiled=True)
    d_normed = lax.dot_general(
        d_projected, full_weight, (((1,), (1,)), ((), ())), preferred_element_type=jnp.float32
    )
    d_unit = d_normed * norm_gain
    d_hidden = (
        inv_rms * (d_unit - unit_rows * jnp.mean(d_unit * unit_rows, axis=1, keepdims=True))
    ).astype(jnp.bfloat16)
    grad_scale = 1.0 / math.sqrt(tok_rows * roll_size * fsdp_size)
    share = lax.dot_general(
        normed_columns, plane_d, (((0,), (0,)), ((), ())), preferred_element_type=jnp.float32
    )
    pieces = lax.all_to_all(
        share.reshape(roll_size, -1, share.shape[1]), "roll", split_axis=0, concat_axis=0, tiled=True
    )
    kv_grad = lax.all_gather(
        jnp.sum(pieces, axis=0) * grad_scale, "roll", axis=0, tiled=True
    )
    return (d_queries, d_hidden, kv_grad)


def solution(mesh):
    placed = (
        P(("roll", "fsdp"), None),
        P("fsdp", None, None),
        P(("roll", "fsdp"), None),
        P(("roll", "fsdp"), None),
        P(),
        P("fsdp", None),
        P(("roll", "fsdp"), None),
        P(("roll", "fsdp"), None),
        P(("roll", "fsdp"), None),
        P(("roll", "fsdp"), None),
        P(("roll", "fsdp"), None),
    )
    return jax.shard_map(
        shards,
        mesh=mesh,
        in_specs=placed,
        out_specs=(P(("roll", "fsdp"), None), P(("roll", "fsdp"), None), P("fsdp", None)),
        check_vma=False,
    )
```

```python
import functools
import math

import jax
import jax.numpy as jnp
from jax import lax
from jax.experimental import pallas as pl
from jax.experimental.pallas import tpu as pltpu
from jax.sharding import PartitionSpec as P

KV = 4
HD = 128
GROUP = 8
D = 4096
ROWS = 128
KVW = KV * HD
SIDE = 4
CHIPS = SIDE * SIDE
ROLL = 8
SLOT = 24
PACKED = ROLL * 2 * SLOT
CHIP_COLS = D // CHIPS
SLICE = 2 * ROWS // ROLL
CHUNKS = 1

ratio_cap = 2.0
norm_eps = 1e-06
MESH = pl.DeviceIdType.MESH
F32 = jnp.float32
BF16 = jnp.bfloat16


def dot(a, b, dims=((1,), (0,))):
    return lax.dot_general(a, b, (dims, ((), ())), preferred_element_type=F32)


class Gather:
    def __init__(self, buf, send_sem, recv_sem, x, y, core):
        self.buf, self.send_sem, self.recv_sem = buf, send_sem, recv_sem
        self.x, self.y, self.core = x, y, core
        self.started = []

    def at(self, half, du, dv):
        dx, dy = (du, dv) if half == 0 else (dv, du)
        chip = lax.rem(self.y + dy + SIDE, SIDE) * SIDE + lax.rem(self.x + dx + SIDE, SIDE)
        return chip * 2 + self.core, chip

    def view(self, half, du, dv, quarter):
        ref = self.buf.at[self.at(half, du, dv)[1], half]
        return ref if quarter is None else ref.at[pl.ds(quarter * (ROWS // 2), ROWS // 2)]

    def send(self, half, block, step, sem, quarter=None):
        n = len(self.started)
        ref = self.view(half, *block, quarter)
        copy = pltpu.make_async_remote_copy(
            src_ref=ref,
            dst_ref=ref,
            send_sem=self.send_sem.at[n],
            recv_sem=self.recv_sem.at[half, sem],
            device_id={"fsdp": self.at(half, *step)[0]},
            device_id_type=MESH,
        )
        copy.start()
        self.started.append(copy)

    def arrive(self, half, block, sem, quarter=None):
        ref = self.view(half, *block, quarter)
        pltpu.make_async_copy(ref, ref, self.recv_sem.at[half, sem]).wait()

    def own(self, half):
        self.send(half, (0, 0), (1, 0), 0)
        self.send(half, (0, 0), (-1, 0), 1)
        self.second(half, 0)

    def second(self, half, j):
        du = (0, -1, 1, 2)[j]
        self.send(half, (du, 0), (0, 1), 4 + 4 * j)
        self.send(half, (du, 0), (0, -1), 5 + 4 * j)

    def first_near(self, half):
        self.arrive(half, (-1, 0), 0)
        self.send(half, (-1, 0), (1, 0), 2, 0)
        self.second(half, 1)
        self.arrive(half, (1, 0), 1)
        self.send(half, (1, 0), (-1, 0), 3, 1)
        self.second(half, 2)

    def first_far(self, half):
        self.arrive(half, (2, 0), 2, 0)
        self.arrive(half, (2, 0), 3, 1)
        self.second(half, 3)

    def second_near(self, half, j):
        du = (0, -1, 1, 2)[j]
        self.arrive(half, (du, -1), 4 + 4 * j)
        self.send(half, (du, -1), (0, 1), 6 + 4 * j, 0)
        self.arrive(half, (du, 1), 5 + 4 * j)
        self.send(half, (du, 1), (0, -1), 7 + 4 * j, 1)

    def second_far(self, half, j):
        du = (0, -1, 1, 2)[j]
        self.arrive(half, (du, 2), 6 + 4 * j, 0)
        self.arrive(half, (du, 2), 7 + 4 * j, 1)

    def finish(self):
        for copy in self.started:
            copy.wait_send()


def starts_of(counts):
    total, out = jnp.int32(0), []
    for count in counts:
        out.append(total)
        total = total + count
    return out


def selection(counts, across):
    starts = starts_of(counts)
    shape = (1, PACKED) if across else (PACKED, 1)
    place = lax.broadcasted_iota(jnp.int32, shape, 1 if across else 0)
    target = jnp.full(shape, -1, jnp.int32)
    for s in range(ROLL):
        for half in range(2):
            first = (2 * s + half) * SLOT
            inside = (place >= first) & (place < first + counts[s])
            inside = inside & (place < first + SLOT)
            target = jnp.where(inside, place + (starts[s] + (half * ROWS - first)), target)
    full = (2 * ROWS, PACKED) if across else (PACKED, 2 * ROWS)
    row = lax.broadcasted_iota(jnp.int32, full, 0 if across else 1)
    return jnp.where(row == target, 1.0, 0.0).astype(BF16)


def column_of(row):
    return jnp.transpose(jnp.broadcast_to(row, (ROWS, ROWS)))


def body(
    hid, cnt, qry, ups, gain, wgt, lpn, lpo, adv, seg, trm,
    dq_out, dh_out, kg_out,
    hv, qv, uv, dqv, dhv, nb, dn, wbuf, wother, dbuf, ncols, acc, kvx, kvown, dkvown,
    pack_s, pack_r, unpack_s, unpack_r, pk, rv, pk2, rv2, inv, bias, coef, ps, rs, rd, og, kgv,
    local_sem, pair_send, pair_recv, w_send, w_recv, d_send, d_recv,
    n_send, n_recv, z_send, z_recv, b_send, b_recv, r_send, r_recv, o_send, o_recv,
):
    z = lax.axis_index("roll")
    f = lax.axis_index("fsdp")
    core = lax.rem(f, 2)
    other = 1 - core
    chip = f // 2
    x = lax.rem(chip, SIDE)
    y = chip // SIDE
    partner = chip * 2 + other

    barrier = pltpu.get_barrier_semaphore()
    pl.semaphore_signal(barrier, inc=1, device_id={"fsdp": partner}, device_id_type=MESH)
    for d in range(1, CHIPS):
        peer = lax.rem(chip + d, CHIPS) * 2 + core
        pl.semaphore_signal(barrier, inc=1, device_id={"fsdp": peer}, device_id_type=MESH)
    for d in range(1, ROLL):
        for who in (f, partner):
            pl.semaphore_signal(
                barrier, inc=1, device_id={"roll": lax.rem(z + d, ROLL), "fsdp": who}, device_id_type=MESH
            )

    def local(src, dst, n):
        copy = pltpu.make_async_copy(src, dst, local_sem.at[n])
        copy.start()
        return copy

    pair_copies = []

    def to_partner(src, dst, n):
        copy = pltpu.make_async_remote_copy(
            src_ref=src, dst_ref=dst, send_sem=pair_send.at[n], recv_sem=pair_recv.at[n],
            device_id={"fsdp": partner}, device_id_type=MESH,
        )
        copy.start()
        pair_copies.append(copy)

    def from_partner(dst, n):
        pltpu.make_async_copy(dst, dst, pair_recv.at[n]).wait()

    mine = pl.ds(pl.multiple_of(core * KVW, KVW), KVW)
    theirs = pl.ds(pl.multiple_of(other * KVW, KVW), KVW)
    w_copy = local(wgt.at[:, mine], wbuf.at[chip, core], 0)
    h_copy = local(hid, hv, 1)
    q_copy = local(qry, qv, 2)
    u_copy = local(ups, uv, 3)

    pl.semaphore_wait(barrier, 1 + (CHIPS - 1) + 2 * (ROLL - 1))

    to_partner(wgt.at[:, theirs], wbuf.at[chip, core], 0)
    w_copy.wait()
    gather = Gather(wbuf, w_send, w_recv, x, y, core)

    def by_owner(do):
        do(0)
        do(1)

    from_partner(wbuf.at[chip, other], 0)
    by_owner(gather.own)

    h_copy.wait()
    square = jnp.zeros((ROWS, HD), F32)
    for c in range(D // HD):
        part = hv[:, c * HD:(c + 1) * HD].astype(F32)
        square = square + part * part
    inv_rms = lax.rsqrt(jnp.sum(square, axis=1, keepdims=True) * (1.0 / D) + norm_eps)
    inv[...] = jnp.broadcast_to(inv_rms, (ROWS, HD))
    for c in range(CHIPS):
        cols = slice(c * CHIP_COLS, (c + 1) * CHIP_COLS)
        nb[core, :, cols] = (hv[:, cols].astype(F32) * inv_rms * gain[:, cols]).astype(BF16)
    to_partner(nb.at[core], nb.at[core], 1)

    gather.first_near(0)
    gather.first_near(1)

    n_copies = []
    for d in range(1, CHIPS):
        to = lax.rem(chip + d, CHIPS)
        copy = pltpu.make_async_remote_copy(
            src_ref=nb.at[core, :, pl.ds(pl.multiple_of(to * CHIP_COLS, CHIP_COLS), CHIP_COLS)],
            dst_ref=ncols.at[chip, core],
            send_sem=n_send.at[d], recv_sem=n_recv.at[d],
            device_id={"fsdp": to * 2 + core}, device_id_type=MESH,
        )
        n_copies.append(copy)

    send_counts = [cnt[0, z, l] for l in range(ROLL)]
    recv_counts = [cnt[0, s, z] for s in range(ROLL)]
    unpack_s[...] = selection(send_counts, True)
    unpack_r[...] = selection(recv_counts, True)
    pack_s[...] = selection(send_counts, False)
    pack_r[...] = selection(recv_counts, False)
    segment = seg[...]
    picked = jnp.zeros((1, ROWS), F32)
    for r in range(4):
        picked = picked + jnp.where(segment == r, adv[0, r], 0.0)
    weight = trm[...].astype(F32) * picked * jnp.minimum(jnp.exp(lpn[...] - lpo[...]), ratio_cap)
    coef[...] = column_of(weight)
    row = lax.broadcasted_iota(jnp.int32, (ROWS, ROWS), 0)
    col = lax.broadcasted_iota(jnp.int32, (ROWS, ROWS), 1)
    segment_f = segment.astype(F32)
    same = column_of(segment_f) == jnp.broadcast_to(segment_f, (ROWS, ROWS))
    bias[...] = jnp.where(same & (col <= row), 0.0, -jnp.inf)

    gather.second_near(0, 0)
    gather.second_near(1, 0)
    gather.first_far(0)
    gather.first_far(1)

    def project(c, first=False):
        cols = pl.ds(pl.multiple_of(c * CHIP_COLS, CHIP_COLS), CHIP_COLS)
        left = nb[:, :, cols].reshape(2 * ROWS, CHIP_COLS)
        term = dot(left, wbuf[c].reshape(2 * ROWS, KVW))
        if first:
            acc[...] = term
        else:
            acc[...] += term

    def chip_at(dx, dy):
        return lax.rem(y + dy + SIDE, SIDE) * SIDE + lax.rem(x + dx + SIDE, SIDE)

    from_partner(nb.at[other], 1)
    project(chip, True)
    for dx, dy in ((1, 0), (-1, 0), (0, 1), (0, -1)):
        project(chip_at(dx, dy))
    for j in (1, 2):
        gather.second_near(0, j)
        gather.second_near(1, j)
    for dx, dy in ((1, 1), (-1, 1), (1, -1), (-1, -1)):
        project(chip_at(dx, dy))
    gather.second_near(0, 3)
    gather.second_near(1, 3)
    gather.second_far(0, 0)
    gather.second_far(1, 0)
    for dx, dy in ((2, 0), (0, 2)):
        project(chip_at(dx, dy))
    for j in (1, 2):
        gather.second_far(0, j)
        gather.second_far(1, j)
    for dx, dy in ((2, 1), (2, -1), (1, 2), (-1, 2)):
        project(chip_at(dx, dy))
    gather.second_far(0, 3)
    gather.second_far(1, 3)
    project(chip_at(2, 2))

    for r in range(2):
        kvx[r] = acc[r * ROWS:(r + 1) * ROWS, :].astype(BF16)
    to_partner(kvx.at[other], kvown.at[core], 2)
    kvown[core] = kvx[core]
    to_partner(wbuf, wother, 3)
    for copy in n_copies:
        copy.start()
    n_own = local(
        nb.at[core, :, pl.ds(pl.multiple_of(chip * CHIP_COLS, CHIP_COLS), CHIP_COLS)],
        ncols.at[chip, core], 4,
    )
    from_partner(kvown.at[other], 2)

    def heads(ref, h):
        cols = slice(h * HD, (h + 1) * HD)
        return jnp.concatenate([ref[0, :, cols], ref[1, :, cols]], axis=0)

    z_copies = []

    def relay(out_buf, in_buf, send_sem, recv_sem, h):
        for d in range(1, ROLL):
            to = lax.rem(z + d, ROLL)
            copy = pltpu.make_async_remote_copy(
                src_ref=out_buf.at[h, to], dst_ref=in_buf.at[h, z],
                send_sem=send_sem.at[h, d], recv_sem=recv_sem.at[h, d],
                device_id={"roll": to}, device_id_type=MESH,
            )
            copy.start()
            z_copies.append(copy)
        in_buf[h, z] = out_buf[h, z]

    def relayed(in_buf, recv_sem, h):
        for d in range(1, ROLL):
            ref = in_buf.at[h, lax.rem(z + ROLL - d, ROLL)]
            pltpu.make_async_copy(ref, ref, recv_sem.at[h, d]).wait()

    for h in range(KV):
        packed = dot(pack_s[...], heads(kvown, h)).astype(BF16)
        pk[h] = packed.reshape(ROLL, 2 * SLOT, HD)
        relay(pk, rv, z_send, z_recv, h)

    q_copy.wait()
    u_copy.wait()
    scale = 1.0 / math.sqrt(HD)
    stacked = (GROUP, ROWS, ROWS)
    dq_copies = []
    for h in range(KV):
        relayed(rv, z_recv, h)
        kv = dot(unpack_r[...], rv[h].reshape(PACKED, HD)).astype(BF16)
        keys, values = kv[:ROWS], kv[ROWS:]
        base = h * GROUP * HD
        q = jnp.concatenate([qv[:, base + g * HD:base + (g + 1) * HD] for g in range(GROUP)], axis=0)
        d_out = jnp.concatenate(
            [
                (coef[...] * uv[:, base + g * HD:base + (g + 1) * HD].astype(F32)).astype(BF16)
                for g in range(GROUP)
            ],
            axis=0,
        )
        scores = dot(q, keys, ((1,), (1,))).reshape(stacked) * scale + bias[...][None]
        d_probs = dot(d_out, values, ((1,), (1,))).reshape(stacked)
        expo = jnp.exp(scores - jnp.max(scores, axis=2, keepdims=True))
        probs = expo * (1.0 / jnp.sum(expo, axis=2, keepdims=True))
        probs_low = probs.astype(BF16)
        row_delta = jnp.sum(probs_low.astype(F32) * d_probs, axis=2, keepdims=True)
        d_scores = (probs * (d_probs - row_delta) * scale).astype(BF16)
        d_scores = d_scores.reshape(GROUP * ROWS, ROWS)
        probs_low = probs_low.reshape(GROUP * ROWS, ROWS)
        d_keys = dot(d_scores, q, ((0,), (0,)))
        d_values = dot(probs_low, d_out, ((0,), (0,)))
        d_rows = jnp.concatenate([d_keys, d_values], axis=0).astype(BF16)
        pk2[h] = dot(pack_r[...], d_rows).astype(BF16).reshape(ROLL, 2 * SLOT, HD)
        relay(pk2, rv2, b_send, b_recv, h)
        d_q = dot(d_scores, keys).astype(BF16)
        for g in range(GROUP):
            dqv[:, base + g * HD:base + (g + 1) * HD] = d_q[g * ROWS:(g + 1) * ROWS]
        dq_copies.append(
            local(dqv.at[:, pl.ds(base, GROUP * HD)], dq_out.at[:, pl.ds(base, GROUP * HD)], 5 + h)
        )

    for d in range(1, CHIPS):
        ref = ncols.at[lax.rem(chip + CHIPS - d, CHIPS), core]
        pltpu.make_async_copy(ref, ref, n_recv.at[d]).wait()
    n_own.wait()
    to_partner(ncols.at[:, core], ncols.at[:, core], 4)

    for h in range(KV):
        relayed(rv2, b_recv, h)
        back = dot(unpack_s[...], rv2[h].reshape(PACKED, HD)).astype(BF16)
        cols = slice(h * HD, (h + 1) * HD)
        dkvown[0, :, cols] = back[:ROWS]
        dkvown[1, :, cols] = back[ROWS:]
    to_partner(dkvown.at[other], dbuf.at[chip, core], 5)
    dbuf[chip, core] = dkvown[core]
    from_partner(dbuf.at[chip, other], 5)
    back = Gather(dbuf, d_send, d_recv, x, y, core)
    by_owner(back.own)
    from_partner(ncols.at[:, other], 4)
    from_partner(wother, 3)

    moment = [jnp.zeros((ROWS, HD), F32)]

    def row_grad(c):
        cols = slice(c * CHIP_COLS, (c + 1) * CHIP_COLS)
        d_n = dot(dkvown[core], wbuf[c].reshape(2 * ROWS, KVW), ((1,), (1,)))
        d_n = d_n + dot(dkvown[other], wother[c].reshape(2 * ROWS, KVW), ((1,), (1,)))
        d_n = d_n * gain[:, cols]
        dn[:, cols] = d_n
        for i in range(CHIP_COLS // HD):
            lanes = slice(c * CHIP_COLS + i * HD, c * CHIP_COLS + (i + 1) * HD)
            unit = hv[:, lanes].astype(F32) * inv[...]
            moment[0] = moment[0] + d_n[:, i * HD:(i + 1) * HD] * unit

    def row_out():
        mean = jnp.sum(moment[0], axis=1, keepdims=True) * (1.0 / D)
        inv_rms = inv[:, :1]
        for c in range(CHIPS):
            cols = slice(c * CHIP_COLS, (c + 1) * CHIP_COLS)
            unit = hv[:, cols].astype(F32) * inv_rms
            dhv[:, cols] = (inv_rms * (dn[:, cols] - unit * mean)).astype(BF16)
        return local(dhv, dh_out, 9)

    def grad(c, first=False):
        left = ncols[c].reshape(2 * ROWS, CHIP_COLS)
        term = dot(left, dbuf[c].reshape(2 * ROWS, KVW), ((0,), (0,)))
        if first:
            acc[...] = term
        else:
            acc[...] += term

    for c in range(0, 4):
        row_grad(c)
    back.first_near(0)
    back.first_near(1)
    for c in range(4, 8):
        row_grad(c)
    back.second_near(0, 0)
    back.second_near(1, 0)
    back.first_far(0)
    back.first_far(1)
    for c in range(8, 12):
        row_grad(c)
    grad(chip, True)
    for j in (1, 2):
        back.second_near(0, j)
        back.second_near(1, j)
    for c in range(12, 16):
        row_grad(c)
    for dx, dy in ((1, 0), (-1, 0), (0, 1), (0, -1)):
        grad(chip_at(dx, dy))
    back.second_near(0, 3)
    back.second_near(1, 3)
    dh_copy = row_out()
    for dx, dy in ((1, 1), (-1, 1), (1, -1), (-1, -1)):
        grad(chip_at(dx, dy))
    back.second_far(0, 0)
    back.second_far(1, 0)
    for dx, dy in ((2, 0), (0, 2)):
        grad(chip_at(dx, dy))
    for j in (1, 2):
        back.second_far(0, j)
        back.second_far(1, j)
    for dx, dy in ((2, 1), (2, -1), (1, 2), (-1, 2)):
        grad(chip_at(dx, dy))
    back.second_far(0, 3)
    back.second_far(1, 3)
    grad(chip_at(2, 2))

    grad_scale = 1.0 / math.sqrt(ROWS * 2 * CHIPS * ROLL)
    ps[...] = (acc[...] * grad_scale).astype(BF16).reshape(ROLL, SLICE, KVW)
    last = []
    for d in range(1, ROLL):
        to = lax.rem(z + d, ROLL)
        copy = pltpu.make_async_remote_copy(
            src_ref=ps.at[to], dst_ref=rs.at[z],
            send_sem=r_send.at[d], recv_sem=r_recv.at[d],
            device_id={"roll": to}, device_id_type=MESH,
        )
        copy.start()
        last.append(copy)
    rs[z] = ps[z]
    for d in range(1, ROLL):
        ref = rs.at[lax.rem(z + ROLL - d, ROLL)]
        pltpu.make_async_copy(ref, ref, r_recv.at[d]).wait()
    total = rs[0].astype(F32)
    for s in range(1, ROLL):
        total = total + rs[s].astype(F32)
    rd[...] = total.astype(BF16)
    owner = z // (ROLL // 2)
    place = lax.rem(z, ROLL // 2)

    def hand_over(to, d):
        return pltpu.make_async_remote_copy(
            src_ref=rd, dst_ref=og.at[core, place],
            send_sem=o_send.at[d], recv_sem=o_recv.at[core, place],
            device_id={"roll": to, "fsdp": chip * 2 + owner}, device_id_type=MESH,
        )

    for d in range(1, ROLL):
        copy = hand_over(lax.rem(z + d, ROLL), d)
        copy.start()
        last.append(copy)

    @pl.when(owner != core)
    def _():
        hand_over(z, 0).start()

    @pl.when(owner == core)
    def _():
        og[core, place] = rd[...]

    for s in range(ROLL // 2):
        for k in range(2):
            ref = og.at[k, s]
            own = (core * (ROLL // 2) + s == z) & (core == k)

            @pl.when(jnp.logical_not(own))
            def _():
                pltpu.make_async_copy(ref, ref, o_recv.at[k, s]).wait()

    for k in range(2):
        kgv[:, k * KVW:(k + 1) * KVW] = og[k].astype(F32).reshape(ROWS, KVW)
    kg_copy = local(kgv, kg_out, 10)

    @pl.when(owner != core)
    def _():
        hand_over(z, 0).wait_send()

    gather.finish()
    back.finish()
    for copy in pair_copies + n_copies + z_copies + last:
        copy.wait_send()
    for copy in dq_copies:
        copy.wait()
    dh_copy.wait()
    kg_copy.wait()


def shards(
    hidden, send_counts, queries, upstream, norm_gain, kv_weight,
    logp_new, logp_old, advantage, segment_ids, trim_mask,
):
    anywhere = pl.BlockSpec(memory_space=pl.ANY)
    vmem = pl.BlockSpec(memory_space=pltpu.VMEM)
    smem = pl.BlockSpec(memory_space=pltpu.SMEM)
    dma = pltpu.SemaphoreType.DMA
    relay_buf = pltpu.VMEM((KV, ROLL, 2 * SLOT, HD), BF16)
    rows = pltpu.VMEM((ROWS, D), BF16)
    return pl.pallas_call(
        body,
        out_shape=(
            jax.ShapeDtypeStruct((ROWS, D), BF16),
            jax.ShapeDtypeStruct((ROWS, D), BF16),
            jax.ShapeDtypeStruct((ROWS, 2 * KVW), F32),
        ),
        in_specs=[anywhere, smem, anywhere, anywhere, vmem, anywhere, vmem, vmem, smem, vmem, vmem],
        out_specs=(anywhere, anywhere, anywhere),
        scratch_shapes=[
            rows, rows, rows, rows, rows,
            pltpu.VMEM((2, ROWS, D), BF16),
            pltpu.VMEM((ROWS, D), F32),
            pltpu.VMEM((CHIPS, 2, ROWS, KVW), BF16),
            pltpu.VMEM((CHIPS, 2, ROWS, KVW), BF16),
            pltpu.VMEM((CHIPS, 2, ROWS, KVW), BF16),
            pltpu.VMEM((CHIPS, 2, ROWS, CHIP_COLS), BF16),
            pltpu.VMEM((2 * ROWS, KVW), F32),
            pltpu.VMEM((2, ROWS, KVW), BF16),
            pltpu.VMEM((2, ROWS, KVW), BF16),
            pltpu.VMEM((2, ROWS, KVW), BF16),
            pltpu.VMEM((PACKED, 2 * ROWS), BF16),
            pltpu.VMEM((PACKED, 2 * ROWS), BF16),
            pltpu.VMEM((2 * ROWS, PACKED), BF16),
            pltpu.VMEM((2 * ROWS, PACKED), BF16),
            relay_buf, relay_buf, relay_buf, relay_buf,
            pltpu.VMEM((ROWS, HD), F32),
            pltpu.VMEM((ROWS, ROWS), F32),
            pltpu.VMEM((ROWS, ROWS), F32),
            pltpu.VMEM((ROLL, SLICE, KVW), BF16),
            pltpu.VMEM((ROLL, SLICE, KVW), BF16),
            pltpu.VMEM((SLICE, KVW), BF16),
            pltpu.VMEM((2, ROLL // 2, SLICE, KVW), BF16),
            pltpu.VMEM((ROWS, 2 * KVW), F32),
            dma((11,)), dma((6,)), dma((6,)),
            dma((40,)), dma((2, 20)), dma((40,)), dma((2, 20)),
            dma((CHIPS,)), dma((CHIPS,)),
            dma((KV, ROLL)), dma((KV, ROLL)), dma((KV, ROLL)), dma((KV, ROLL)),
            dma((ROLL,)), dma((ROLL,)), dma((ROLL,)), dma((2, ROLL // 2)),
        ],
        compiler_params=pltpu.CompilerParams(
            collective_id=0, has_side_effects=True, vmem_limit_bytes=60 << 20
        ),
        name="backward",
    )(
        hidden, send_counts, queries, upstream, norm_gain.reshape(1, D), kv_weight,
        logp_new, logp_old, advantage, segment_ids, trim_mask,
    )


def solution(mesh):
    placed = (
        P(("roll", "fsdp"), None),
        P("fsdp", None, None),
        P(("roll", "fsdp"), None),
        P(("roll", "fsdp"), None),
        P(),
        P("fsdp", None),
        P(("roll", "fsdp"), None),
        P(("roll", "fsdp"), None),
        P(("roll", "fsdp"), None),
        P(("roll", "fsdp"), None),
        P(("roll", "fsdp"), None),
    )
    return jax.shard_map(
        shards,
        mesh=mesh,
        in_specs=placed,
        out_specs=(P(("roll", "fsdp"), None), P(("roll", "fsdp"), None), P("fsdp", None)),
        check_vma=False,
    )
```

```python
import functools
import math

import jax
import jax.numpy as jnp
from jax import lax
from jax.experimental import pallas as pl
from jax.experimental.pallas import tpu as pltpu
from jax.sharding import PartitionSpec as P

KV = 4
HD = 128
GROUP = 8
D = 4096
ROWS = 128
KVW = KV * HD
SIDE = 4
CHIPS = SIDE * SIDE
ROLL = 8
SLOT = 24
PACKED = ROLL * 2 * SLOT
CHIP_COLS = D // CHIPS
SLICE = 2 * ROWS // ROLL
D_CHUNKS = 2
WIDTH = KVW // D_CHUNKS
PIECES = 4

ratio_cap = 2.0
norm_eps = 1e-06
MESH = pl.DeviceIdType.MESH
F32 = jnp.float32
BF16 = jnp.bfloat16


def dot(a, b, dims=((1,), (0,))):
    return lax.dot_general(a, b, (dims, ((), ())), preferred_element_type=F32)


class Gather:
    def __init__(self, buf, send_sem, recv_sem, x, y, core, cols=slice(0, KVW)):
        self.cols = pl.ds(cols.start, cols.stop - cols.start)
        self.buf, self.send_sem, self.recv_sem = buf, send_sem, recv_sem
        self.x, self.y, self.core = x, y, core
        self.started = []

    def at(self, half, du, dv):
        dx, dy = (du, dv) if half == 0 else (dv, du)
        chip = lax.rem(self.y + dy + SIDE, SIDE) * SIDE + lax.rem(self.x + dx + SIDE, SIDE)
        return chip * 2 + self.core, chip

    def view(self, half, du, dv, quarter):
        rows = pl.ds(0, ROWS) if quarter is None else pl.ds(quarter * (ROWS // 2), ROWS // 2)
        return self.buf.at[self.at(half, du, dv)[1], half, rows, self.cols]

    def send(self, half, block, step, sem, quarter=None):
        n = len(self.started)
        ref = self.view(half, *block, quarter)
        copy = pltpu.make_async_remote_copy(
            src_ref=ref,
            dst_ref=ref,
            send_sem=self.send_sem.at[n],
            recv_sem=self.recv_sem.at[half, sem],
            device_id={"fsdp": self.at(half, *step)[0]},
            device_id_type=MESH,
        )
        copy.start()
        self.started.append(copy)

    def arrive(self, half, block, sem, quarter=None):
        ref = self.view(half, *block, quarter)
        pltpu.make_async_copy(ref, ref, self.recv_sem.at[half, sem]).wait()

    def own(self, half):
        self.send(half, (0, 0), (1, 0), 0)
        self.send(half, (0, 0), (-1, 0), 1)
        self.second(half, 0)

    def second(self, half, j):
        du = (0, -1, 1, 2)[j]
        self.send(half, (du, 0), (0, 1), 4 + 4 * j)
        self.send(half, (du, 0), (0, -1), 5 + 4 * j)

    def first_near(self, half):
        self.arrive(half, (-1, 0), 0)
        self.send(half, (-1, 0), (1, 0), 2, 0)
        self.second(half, 1)
        self.arrive(half, (1, 0), 1)
        self.send(half, (1, 0), (-1, 0), 3, 1)
        self.second(half, 2)

    def first_far(self, half):
        self.arrive(half, (2, 0), 2, 0)
        self.arrive(half, (2, 0), 3, 1)
        self.second(half, 3)

    def second_near(self, half, j):
        du = (0, -1, 1, 2)[j]
        self.arrive(half, (du, -1), 4 + 4 * j)
        self.send(half, (du, -1), (0, 1), 6 + 4 * j, 0)
        self.arrive(half, (du, 1), 5 + 4 * j)
        self.send(half, (du, 1), (0, -1), 7 + 4 * j, 1)

    def second_far(self, half, j):
        du = (0, -1, 1, 2)[j]
        self.arrive(half, (du, 2), 6 + 4 * j, 0)
        self.arrive(half, (du, 2), 7 + 4 * j, 1)

    def finish(self):
        for copy in self.started:
            copy.wait_send()


def starts_of(counts):
    total, out = jnp.int32(0), []
    for count in counts:
        out.append(total)
        total = total + count
    return out


def selection(counts, across):
    starts = starts_of(counts)
    shape = (1, PACKED) if across else (PACKED, 1)
    place = lax.broadcasted_iota(jnp.int32, shape, 1 if across else 0)
    target = jnp.full(shape, -1, jnp.int32)
    for s in range(ROLL):
        for half in range(2):
            first = (2 * s + half) * SLOT
            inside = (place >= first) & (place < first + counts[s])
            inside = inside & (place < first + SLOT)
            target = jnp.where(inside, place + (starts[s] + (half * ROWS - first)), target)
    full = (2 * ROWS, PACKED) if across else (PACKED, 2 * ROWS)
    row = lax.broadcasted_iota(jnp.int32, full, 0 if across else 1)
    return jnp.where(row == target, 1.0, 0.0).astype(BF16)


def column_of(row):
    return jnp.transpose(jnp.broadcast_to(row, (ROWS, ROWS)))


def body(
    hid, cnt, qry, ups, gain, wgt, lpn, lpo, adv, seg, trm,
    dq_out, dh_out, kg_out,
    hv, qv, uv, dqv, dhv, nb, dn, wbuf, wother, dbuf, ncols, acc, kvx, kvown, dkvown,
    pack_s, pack_r, unpack_s, unpack_r, pk, rv, pk2, rv2, inv, bias, coef, ps, rs, rd, og, kgv,
    local_sem, pair_send, pair_recv, w_send, w_recv, d_send, d_recv,
    n_send, n_recv, z_send, z_recv, b_send, b_recv, r_send, r_recv, o_send, o_recv,
):
    z = lax.axis_index("roll")
    f = lax.axis_index("fsdp")
    core = lax.rem(f, 2)
    other = 1 - core
    chip = f // 2
    x = lax.rem(chip, SIDE)
    y = chip // SIDE
    partner = chip * 2 + other

    barrier = pltpu.get_barrier_semaphore()
    pl.semaphore_signal(barrier, inc=1, device_id={"fsdp": partner}, device_id_type=MESH)
    for d in range(1, CHIPS):
        peer = lax.rem(chip + d, CHIPS) * 2 + core
        pl.semaphore_signal(barrier, inc=1, device_id={"fsdp": peer}, device_id_type=MESH)
    for d in range(1, ROLL):
        for who in (f, partner):
            pl.semaphore_signal(
                barrier, inc=1, device_id={"roll": lax.rem(z + d, ROLL), "fsdp": who}, device_id_type=MESH
            )

    def local(src, dst, n):
        copy = pltpu.make_async_copy(src, dst, local_sem.at[n])
        copy.start()
        return copy

    pair_copies = []

    def to_partner(src, dst, n):
        copy = pltpu.make_async_remote_copy(
            src_ref=src, dst_ref=dst, send_sem=pair_send.at[n], recv_sem=pair_recv.at[n],
            device_id={"fsdp": partner}, device_id_type=MESH,
        )
        copy.start()
        pair_copies.append(copy)

    def from_partner(dst, n):
        pltpu.make_async_copy(dst, dst, pair_recv.at[n]).wait()

    mine = pl.ds(pl.multiple_of(core * KVW, KVW), KVW)
    theirs = pl.ds(pl.multiple_of(other * KVW, KVW), KVW)
    w_copy = local(wgt.at[:, mine], wbuf.at[chip, core], 0)
    h_copy = local(hid, hv, 1)
    q_copy = local(qry, qv, 2)
    u_copy = local(ups, uv, 3)

    pl.semaphore_wait(barrier, 1 + (CHIPS - 1) + 2 * (ROLL - 1))

    to_partner(wgt.at[:, theirs], wbuf.at[chip, core], 0)
    w_copy.wait()
    gather = Gather(wbuf, w_send, w_recv, x, y, core)

    def by_owner(do):
        do(0)
        do(1)

    from_partner(wbuf.at[chip, other], 0)
    by_owner(gather.own)

    h_copy.wait()
    square = jnp.zeros((ROWS, HD), F32)
    for c in range(D // HD):
        part = hv[:, c * HD:(c + 1) * HD].astype(F32)
        square = square + part * part
    inv_rms = lax.rsqrt(jnp.sum(square, axis=1, keepdims=True) * (1.0 / D) + norm_eps)
    inv[...] = jnp.broadcast_to(inv_rms, (ROWS, HD))
    for c in range(CHIPS):
        cols = slice(c * CHIP_COLS, (c + 1) * CHIP_COLS)
        nb[core, :, cols] = (hv[:, cols].astype(F32) * inv_rms * gain[:, cols]).astype(BF16)
    to_partner(nb.at[core], nb.at[core], 1)

    gather.first_near(0)
    gather.first_near(1)

    n_copies = []
    for d in range(1, CHIPS):
        to = lax.rem(chip + d, CHIPS)
        copy = pltpu.make_async_remote_copy(
            src_ref=nb.at[core, :, pl.ds(pl.multiple_of(to * CHIP_COLS, CHIP_COLS), CHIP_COLS)],
            dst_ref=ncols.at[chip, core],
            send_sem=n_send.at[d], recv_sem=n_recv.at[d],
            device_id={"fsdp": to * 2 + core}, device_id_type=MESH,
        )
        n_copies.append(copy)

    send_counts = [cnt[0, z, l] for l in range(ROLL)]
    recv_counts = [cnt[0, s, z] for s in range(ROLL)]
    unpack_s[...] = selection(send_counts, True)
    unpack_r[...] = selection(recv_counts, True)
    pack_s[...] = selection(send_counts, False)
    pack_r[...] = selection(recv_counts, False)
    segment = seg[...]
    picked = jnp.zeros((1, ROWS), F32)
    for r in range(4):
        picked = picked + jnp.where(segment == r, adv[0, r], 0.0)
    weight = trm[...].astype(F32) * picked * jnp.minimum(jnp.exp(lpn[...] - lpo[...]), ratio_cap)
    coef[...] = column_of(weight)
    row = lax.broadcasted_iota(jnp.int32, (ROWS, ROWS), 0)
    col = lax.broadcasted_iota(jnp.int32, (ROWS, ROWS), 1)
    segment_f = segment.astype(F32)
    same = column_of(segment_f) == jnp.broadcast_to(segment_f, (ROWS, ROWS))
    bias[...] = jnp.where(same & (col <= row), 0.0, -jnp.inf)

    gather.second_near(0, 0)
    gather.second_near(1, 0)
    gather.first_far(0)
    gather.first_far(1)

    def project(c, first=False):
        cols = pl.ds(pl.multiple_of(c * CHIP_COLS, CHIP_COLS), CHIP_COLS)
        left = nb[:, :, cols].reshape(2 * ROWS, CHIP_COLS)
        term = dot(left, wbuf[c].reshape(2 * ROWS, KVW))
        if first:
            acc[...] = term
        else:
            acc[...] += term

    def chip_at(dx, dy):
        return lax.rem(y + dy + SIDE, SIDE) * SIDE + lax.rem(x + dx + SIDE, SIDE)

    from_partner(nb.at[other], 1)
    project(chip, True)
    for dx, dy in ((1, 0), (-1, 0), (0, 1), (0, -1)):
        project(chip_at(dx, dy))
    for j in (1, 2):
        gather.second_near(0, j)
        gather.second_near(1, j)
    for dx, dy in ((1, 1), (-1, 1), (1, -1), (-1, -1)):
        project(chip_at(dx, dy))
    gather.second_near(0, 3)
    gather.second_near(1, 3)
    gather.second_far(0, 0)
    gather.second_far(1, 0)
    for dx, dy in ((2, 0), (0, 2)):
        project(chip_at(dx, dy))
    for j in (1, 2):
        gather.second_far(0, j)
        gather.second_far(1, j)
    for dx, dy in ((2, 1), (2, -1), (1, 2), (-1, 2)):
        project(chip_at(dx, dy))
    gather.second_far(0, 3)
    gather.second_far(1, 3)
    project(chip_at(2, 2))

    for r in range(2):
        kvx[r] = acc[r * ROWS:(r + 1) * ROWS, :].astype(BF16)
    to_partner(kvx.at[other], kvown.at[core], 2)
    kvown[core] = kvx[core]
    to_partner(wbuf, wother, 3)
    for copy in n_copies:
        copy.start()
    n_own = local(
        nb.at[core, :, pl.ds(pl.multiple_of(chip * CHIP_COLS, CHIP_COLS), CHIP_COLS)],
        ncols.at[chip, core], 4,
    )
    from_partner(kvown.at[other], 2)

    def heads(ref, h):
        cols = slice(h * HD, (h + 1) * HD)
        return jnp.concatenate([ref[0, :, cols], ref[1, :, cols]], axis=0)

    z_copies = []

    def relay(out_buf, in_buf, send_sem, recv_sem, h):
        for d in range(1, ROLL):
            to = lax.rem(z + d, ROLL)
            copy = pltpu.make_async_remote_copy(
                src_ref=out_buf.at[h, to], dst_ref=in_buf.at[h, z],
                send_sem=send_sem.at[h, d], recv_sem=recv_sem.at[h, d],
                device_id={"roll": to}, device_id_type=MESH,
            )
            copy.start()
            z_copies.append(copy)
        in_buf[h, z] = out_buf[h, z]

    def relayed(in_buf, recv_sem, h):
        for d in range(1, ROLL):
            ref = in_buf.at[h, lax.rem(z + ROLL - d, ROLL)]
            pltpu.make_async_copy(ref, ref, recv_sem.at[h, d]).wait()

    for h in range(KV):
        packed = dot(pack_s[...], heads(kvown, h)).astype(BF16)
        pk[h] = packed.reshape(ROLL, 2 * SLOT, HD)
        relay(pk, rv, z_send, z_recv, h)

    q_copy.wait()
    u_copy.wait()
    scale = 1.0 / math.sqrt(HD)
    stacked = (GROUP, ROWS, ROWS)
    out_copies = []
    for h in range(KV):
        relayed(rv, z_recv, h)
        kv = dot(unpack_r[...], rv[h].reshape(PACKED, HD)).astype(BF16)
        keys, values = kv[:ROWS], kv[ROWS:]
        base = h * GROUP * HD
        q = jnp.concatenate([qv[:, base + g * HD:base + (g + 1) * HD] for g in range(GROUP)], axis=0)
        d_out = jnp.concatenate(
            [
                (coef[...] * uv[:, base + g * HD:base + (g + 1) * HD].astype(F32)).astype(BF16)
                for g in range(GROUP)
            ],
            axis=0,
        )
        scores = dot(q, keys, ((1,), (1,))).reshape(stacked) * scale + bias[...][None]
        d_probs = dot(d_out, values, ((1,), (1,))).reshape(stacked)
        expo = jnp.exp(scores - jnp.max(scores, axis=2, keepdims=True))
        probs = expo * (1.0 / jnp.sum(expo, axis=2, keepdims=True))
        probs_low = probs.astype(BF16)
        row_delta = jnp.sum(probs_low.astype(F32) * d_probs, axis=2, keepdims=True)
        d_scores = (probs * (d_probs - row_delta) * scale).astype(BF16)
        d_scores = d_scores.reshape(GROUP * ROWS, ROWS)
        probs_low = probs_low.reshape(GROUP * ROWS, ROWS)
        d_keys = dot(d_scores, q, ((0,), (0,)))
        d_values = dot(probs_low, d_out, ((0,), (0,)))
        d_rows = jnp.concatenate([d_keys, d_values], axis=0).astype(BF16)
        pk2[h] = dot(pack_r[...], d_rows).astype(BF16).reshape(ROLL, 2 * SLOT, HD)
        relay(pk2, rv2, b_send, b_recv, h)
        d_q = dot(d_scores, keys).astype(BF16)
        for g in range(GROUP):
            dqv[:, base + g * HD:base + (g + 1) * HD] = d_q[g * ROWS:(g + 1) * ROWS]
        out_copies.append(
            local(dqv.at[:, pl.ds(base, GROUP * HD)], dq_out.at[:, pl.ds(base, GROUP * HD)], 5 + h)
        )

    def span(g):
        return slice(g * WIDTH, (g + 1) * WIDTH)

    def returned(h):
        relayed(rv2, b_recv, h)
        back = dot(unpack_s[...], rv2[h].reshape(PACKED, HD)).astype(BF16)
        cols = slice(h * HD, (h + 1) * HD)
        dkvown[0, :, cols] = back[:ROWS]
        dkvown[1, :, cols] = back[ROWS:]

    def exchange(g):
        ds = pl.ds(g * WIDTH, WIDTH)
        to_partner(dkvown.at[other, :, ds], dbuf.at[chip, core, :, ds], 5 + g)
        dbuf[chip, core, :, span(g)] = dkvown[core, :, span(g)]

    backs = [
        Gather(dbuf, d_send.at[g], d_recv.at[g], x, y, core, span(g)) for g in range(D_CHUNKS)
    ]

    def begin(g):
        from_partner(dbuf.at[chip, other, :, pl.ds(g * WIDTH, WIDTH)], 5 + g)
        by_owner(backs[g].own)

    returned(0)
    returned(1)
    exchange(0)
    returned(2)
    begin(0)
    returned(3)
    exchange(1)
    for d in range(1, CHIPS):
        ref = ncols.at[lax.rem(chip + CHIPS - d, CHIPS), core]
        pltpu.make_async_copy(ref, ref, n_recv.at[d]).wait()
    n_own.wait()
    begin(1)
    to_partner(ncols.at[:, core], ncols.at[:, core], 4)
    from_partner(wother, 3)

    moment = [jnp.zeros((ROWS, HD), F32)]

    def row_grad(c):
        cols = slice(c * CHIP_COLS, (c + 1) * CHIP_COLS)
        d_n = dot(dkvown[core], wbuf[c].reshape(2 * ROWS, KVW), ((1,), (1,)))
        d_n = d_n + dot(dkvown[other], wother[c].reshape(2 * ROWS, KVW), ((1,), (1,)))
        d_n = d_n * gain[:, cols]
        dn[:, cols] = d_n
        for i in range(CHIP_COLS // HD):
            lanes = slice(c * CHIP_COLS + i * HD, c * CHIP_COLS + (i + 1) * HD)
            unit = hv[:, lanes].astype(F32) * inv[...]
            moment[0] = moment[0] + d_n[:, i * HD:(i + 1) * HD] * unit

    def row_out():
        mean = jnp.sum(moment[0], axis=1, keepdims=True) * (1.0 / D)
        inv_rms = inv[:, :1]
        for c in range(CHIPS):
            cols = slice(c * CHIP_COLS, (c + 1) * CHIP_COLS)
            unit = hv[:, cols].astype(F32) * inv_rms
            dhv[:, cols] = (inv_rms * (dn[:, cols] - unit * mean)).astype(BF16)
        out_copies.append(local(dhv, dh_out, 9))

    def grad(g, *offsets):
        cols = span(g)
        term = None
        for dx, dy in offsets:
            c = chip_at(dx, dy)
            left = ncols[c].reshape(2 * ROWS, CHIP_COLS)
            part = dot(left, dbuf[c, :, :, cols].reshape(2 * ROWS, WIDTH), ((0,), (0,)))
            term = part if term is None else term + part
        if (0, 0) in offsets:
            acc[:, cols] = term
        else:
            acc[:, cols] += term

    near = ((1, 0), (-1, 0), (0, 1), (0, -1))
    corners = ((1, 1), (-1, 1), (1, -1), (-1, -1))
    knights = ((2, 1), (2, -1), (1, 2), (-1, 2))

    def both(do, *args):
        do(0, *args)
        do(1, *args)

    grad_scale = 1.0 / math.sqrt(ROWS * 2 * CHIPS * ROLL)
    owner = z // (ROLL // 2)
    place = lax.rem(z, ROLL // 2)
    last = []

    def scatter(g):
        cols, ds = span(g), pl.ds(g * WIDTH, WIDTH)
        ps[:, :, cols] = (acc[:, cols] * grad_scale).astype(BF16).reshape(ROLL, SLICE, WIDTH)
        for d in range(1, ROLL):
            to = lax.rem(z + d, ROLL)
            copy = pltpu.make_async_remote_copy(
                src_ref=ps.at[to, :, ds], dst_ref=rs.at[z, :, ds],
                send_sem=r_send.at[g, d], recv_sem=r_recv.at[g, d],
                device_id={"roll": to}, device_id_type=MESH,
            )
            copy.start()
            last.append(copy)
        rs[z, :, cols] = ps[z, :, cols]

    def hand_over(to, d, g):
        ds = pl.ds(g * WIDTH, WIDTH)
        return pltpu.make_async_remote_copy(
            src_ref=rd.at[:, ds], dst_ref=og.at[core, place, :, ds],
            send_sem=o_send.at[g, d], recv_sem=o_recv.at[g, core, place],
            device_id={"roll": to, "fsdp": chip * 2 + owner}, device_id_type=MESH,
        )

    def reduce(g):
        cols, ds = span(g), pl.ds(g * WIDTH, WIDTH)
        for d in range(1, ROLL):
            ref = rs.at[lax.rem(z + ROLL - d, ROLL), :, ds]
            pltpu.make_async_copy(ref, ref, r_recv.at[g, d]).wait()
        total = rs[0, :, cols].astype(F32)
        for s in range(1, ROLL):
            total = total + rs[s, :, cols].astype(F32)
        rd[:, cols] = total.astype(BF16)
        for d in range(1, ROLL):
            copy = hand_over(lax.rem(z + d, ROLL), d, g)
            copy.start()
            last.append(copy)

        @pl.when(owner != core)
        def _():
            hand_over(z, 0, g).start()

        @pl.when(owner == core)
        def _():
            og[core, place, :, cols] = rd[:, cols]

    def collect(g):
        cols, ds = span(g), pl.ds(g * WIDTH, WIDTH)
        for s in range(ROLL // 2):
            for k in range(2):
                ref = og.at[k, s, :, ds]
                own = (core * (ROLL // 2) + s == z) & (core == k)

                @pl.when(jnp.logical_not(own))
                def _():
                    pltpu.make_async_copy(ref, ref, o_recv.at[g, k, s]).wait()

        for k in range(2):
            out = slice(k * KVW + cols.start, k * KVW + cols.stop)
            kgv[:, out] = og[k, :, :, cols].astype(F32).reshape(ROWS, WIDTH)

    first, second = backs
    both(first.first_near)
    for c in range(0, 3):
        row_grad(c)
    both(first.second_near, 0)
    both(first.first_far)
    both(second.first_near)
    for c in range(3, 6):
        row_grad(c)
    both(first.second_near, 1)
    both(first.second_near, 2)
    both(second.second_near, 0)
    both(second.first_far)
    from_partner(ncols.at[:, other], 4)
    grad(0, (0, 0), *near)
    both(first.second_near, 3)
    both(second.second_near, 1)
    both(second.second_near, 2)
    grad(0, *corners)
    both(first.second_far, 0)
    grad(0, (2, 0), (0, 2))
    both(first.second_far, 1)
    both(first.second_far, 2)
    grad(0, *knights)
    both(first.second_far, 3)
    grad(0, (2, 2))
    scatter(0)
    both(second.second_near, 3)
    for c in range(6, 16):
        row_grad(c)
    grad(1, (0, 0), *near, *corners)
    row_out()
    both(second.second_far, 0)
    grad(1, (2, 0), (0, 2))
    both(second.second_far, 1)
    both(second.second_far, 2)
    grad(1, *knights)
    both(second.second_far, 3)
    grad(1, (2, 2))
    scatter(1)
    reduce(0)
    reduce(1)
    collect(0)
    collect(1)
    out_copies.append(local(kgv, kg_out, 10))

    @pl.when(owner != core)
    def _():
        for g in range(D_CHUNKS):
            hand_over(z, 0, g).wait_send()

    gather.finish()
    for back in backs:
        back.finish()
    for copy in pair_copies + n_copies + z_copies + last:
        copy.wait_send()
    for copy in out_copies:
        copy.wait()


def store(*refs):
    sources, outs, buffers, (in_sem, out_sem) = refs[:3], refs[3:6], refs[6:9], refs[9:]
    arrivals, leaving = [], []
    rows = ROWS // PIECES
    for piece in range(PIECES):
        part = pl.ds(piece * rows, rows)
        for n in range(3):
            copy = pltpu.make_async_copy(sources[n].at[part], buffers[n].at[part], in_sem.at[n, piece])
            copy.start()
            arrivals.append((copy, n, piece, part))
    for copy, n, piece, part in arrivals:
        copy.wait()
        out = pltpu.make_async_copy(buffers[n].at[part], outs[n].at[part], out_sem.at[n, piece])
        out.start()
        leaving.append(out)
    for out in leaving:
        out.wait()


def shards(
    hidden, send_counts, queries, upstream, norm_gain, kv_weight,
    logp_new, logp_old, advantage, segment_ids, trim_mask,
):
    anywhere = pl.BlockSpec(memory_space=pl.ANY)
    vmem = pl.BlockSpec(memory_space=pltpu.VMEM)
    smem = pl.BlockSpec(memory_space=pltpu.SMEM)
    dma = pltpu.SemaphoreType.DMA
    relay_buf = pltpu.VMEM((KV, ROLL, 2 * SLOT, HD), BF16)
    rows = pltpu.VMEM((ROWS, D), BF16)
    results = pl.pallas_call(
        body,
        out_shape=(
            jax.ShapeDtypeStruct((ROWS, D), BF16),
            jax.ShapeDtypeStruct((ROWS, D), BF16),
            jax.ShapeDtypeStruct((ROWS, 2 * KVW), F32),
        ),
        in_specs=[anywhere, smem, anywhere, anywhere, vmem, anywhere, vmem, vmem, smem, vmem, vmem],
        out_specs=(anywhere, anywhere, anywhere),
        scratch_shapes=[
            rows, rows, rows, rows, rows,
            pltpu.VMEM((2, ROWS, D), BF16),
            pltpu.VMEM((ROWS, D), F32),
            pltpu.VMEM((CHIPS, 2, ROWS, KVW), BF16),
            pltpu.VMEM((CHIPS, 2, ROWS, KVW), BF16),
            pltpu.VMEM((CHIPS, 2, ROWS, KVW), BF16),
            pltpu.VMEM((CHIPS, 2, ROWS, CHIP_COLS), BF16),
            pltpu.VMEM((2 * ROWS, KVW), F32),
            pltpu.VMEM((2, ROWS, KVW), BF16),
            pltpu.VMEM((2, ROWS, KVW), BF16),
            pltpu.VMEM((2, ROWS, KVW), BF16),
            pltpu.VMEM((PACKED, 2 * ROWS), BF16),
            pltpu.VMEM((PACKED, 2 * ROWS), BF16),
            pltpu.VMEM((2 * ROWS, PACKED), BF16),
            pltpu.VMEM((2 * ROWS, PACKED), BF16),
            relay_buf, relay_buf, relay_buf, relay_buf,
            pltpu.VMEM((ROWS, HD), F32),
            pltpu.VMEM((ROWS, ROWS), F32),
            pltpu.VMEM((ROWS, ROWS), F32),
            pltpu.VMEM((ROLL, SLICE, KVW), BF16),
            pltpu.VMEM((ROLL, SLICE, KVW), BF16),
            pltpu.VMEM((SLICE, KVW), BF16),
            pltpu.VMEM((2, ROLL // 2, SLICE, KVW), BF16),
            pltpu.VMEM((ROWS, 2 * KVW), F32),
            dma((11,)), dma((7,)), dma((7,)),
            dma((40,)), dma((2, 20)), dma((D_CHUNKS, 40)), dma((D_CHUNKS, 2, 20)),
            dma((CHIPS,)), dma((CHIPS,)),
            dma((KV, ROLL)), dma((KV, ROLL)), dma((KV, ROLL)), dma((KV, ROLL)),
            dma((D_CHUNKS, ROLL)), dma((D_CHUNKS, ROLL)), dma((D_CHUNKS, ROLL)), dma((D_CHUNKS, 2, ROLL // 2)),
        ],
        compiler_params=pltpu.CompilerParams(
            collective_id=0, has_side_effects=True, vmem_limit_bytes=60 << 20
        ),
        name="backward",
    )(
        hidden, send_counts, queries, upstream, norm_gain.reshape(1, D), kv_weight,
        logp_new, logp_old, advantage, segment_ids, trim_mask,
    )
    return pl.pallas_call(
        store,
        out_shape=tuple(jax.ShapeDtypeStruct(a.shape, a.dtype) for a in results),
        in_specs=[anywhere] * 3,
        out_specs=(anywhere,) * 3,
        scratch_shapes=[pltpu.VMEM(a.shape, a.dtype) for a in results] + [dma((3, PIECES)), dma((3, PIECES))],
        compiler_params=pltpu.CompilerParams(vmem_limit_bytes=60 << 20),
        name="store",
    )(*results)


def solution(mesh):
    placed = (
        P(("roll", "fsdp"), None),
        P("fsdp", None, None),
        P(("roll", "fsdp"), None),
        P(("roll", "fsdp"), None),
        P(),
        P("fsdp", None),
        P(("roll", "fsdp"), None),
        P(("roll", "fsdp"), None),
        P(("roll", "fsdp"), None),
        P(("roll", "fsdp"), None),
        P(("roll", "fsdp"), None),
    )
    return jax.shard_map(
        shards,
        mesh=mesh,
        in_specs=placed,
        out_specs=(P(("roll", "fsdp"), None), P(("roll", "fsdp"), None), P("fsdp", None)),
        check_vma=False,
    )
```

```python
import functools
import math

import jax
import jax.numpy as jnp
from jax import lax
from jax.experimental import pallas as pl
from jax.experimental.pallas import tpu as pltpu
from jax.sharding import PartitionSpec as P

KV = 4
HD = 128
GROUP = 8
D = 4096
ROWS = 128
KVW = KV * HD
SIDE = 4
CHIPS = SIDE * SIDE
ROLL = 8
SLOT = 24
PACKED = ROLL * 2 * SLOT
CHIP_COLS = D // CHIPS
SLICE = 2 * ROWS // ROLL
D_CHUNKS = 2
WIDTH = KVW // D_CHUNKS
PIECES = 4

ratio_cap = 2.0
norm_eps = 1e-06
MESH = pl.DeviceIdType.MESH
F32 = jnp.float32
BF16 = jnp.bfloat16


def dot(a, b, dims=((1,), (0,))):
    return lax.dot_general(a, b, (dims, ((), ())), preferred_element_type=F32)


class Gather:
    def __init__(self, buf, send_sem, recv_sem, x, y, core, cols=slice(0, KVW)):
        self.cols = pl.ds(cols.start, cols.stop - cols.start)
        self.buf, self.send_sem, self.recv_sem = buf, send_sem, recv_sem
        self.x, self.y, self.core = x, y, core
        self.started = []

    def at(self, half, du, dv):
        dx, dy = (du, dv) if half == 0 else (dv, du)
        chip = lax.rem(self.y + dy + SIDE, SIDE) * SIDE + lax.rem(self.x + dx + SIDE, SIDE)
        return chip * 2 + self.core, chip

    def view(self, half, du, dv, quarter):
        rows = pl.ds(0, ROWS) if quarter is None else pl.ds(quarter * (ROWS // 2), ROWS // 2)
        return self.buf.at[self.at(half, du, dv)[1], half, rows, self.cols]

    def send(self, half, block, step, sem, quarter=None):
        n = len(self.started)
        ref = self.view(half, *block, quarter)
        copy = pltpu.make_async_remote_copy(
            src_ref=ref,
            dst_ref=ref,
            send_sem=self.send_sem.at[n],
            recv_sem=self.recv_sem.at[half, sem],
            device_id={"fsdp": self.at(half, *step)[0]},
            device_id_type=MESH,
        )
        copy.start()
        self.started.append(copy)

    def arrive(self, half, block, sem, quarter=None):
        ref = self.view(half, *block, quarter)
        pltpu.make_async_copy(ref, ref, self.recv_sem.at[half, sem]).wait()

    def own(self, half):
        self.send(half, (0, 0), (1, 0), 0)
        self.send(half, (0, 0), (-1, 0), 1)
        self.second(half, 0)

    def second(self, half, j):
        du = (0, -1, 1, 2)[j]
        self.send(half, (du, 0), (0, 1), 4 + 4 * j)
        self.send(half, (du, 0), (0, -1), 5 + 4 * j)

    def first_near(self, half):
        self.arrive(half, (-1, 0), 0)
        self.send(half, (-1, 0), (1, 0), 2, 0)
        self.second(half, 1)
        self.arrive(half, (1, 0), 1)
        self.send(half, (1, 0), (-1, 0), 3, 1)
        self.second(half, 2)

    def first_far(self, half):
        self.arrive(half, (2, 0), 2, 0)
        self.arrive(half, (2, 0), 3, 1)
        self.second(half, 3)

    def second_near(self, half, j):
        du = (0, -1, 1, 2)[j]
        self.arrive(half, (du, -1), 4 + 4 * j)
        self.send(half, (du, -1), (0, 1), 6 + 4 * j, 0)
        self.arrive(half, (du, 1), 5 + 4 * j)
        self.send(half, (du, 1), (0, -1), 7 + 4 * j, 1)

    def second_far(self, half, j):
        du = (0, -1, 1, 2)[j]
        self.arrive(half, (du, 2), 6 + 4 * j, 0)
        self.arrive(half, (du, 2), 7 + 4 * j, 1)

    def finish(self):
        for copy in self.started:
            copy.wait_send()


def starts_of(counts):
    total, out = jnp.int32(0), []
    for count in counts:
        out.append(total)
        total = total + count
    return out


def selection(counts, across):
    starts = starts_of(counts)
    shape = (1, PACKED) if across else (PACKED, 1)
    place = lax.broadcasted_iota(jnp.int32, shape, 1 if across else 0)
    target = jnp.full(shape, -1, jnp.int32)
    for s in range(ROLL):
        for half in range(2):
            first = (2 * s + half) * SLOT
            inside = (place >= first) & (place < first + counts[s])
            inside = inside & (place < first + SLOT)
            target = jnp.where(inside, place + (starts[s] + (half * ROWS - first)), target)
    full = (2 * ROWS, PACKED) if across else (PACKED, 2 * ROWS)
    row = lax.broadcasted_iota(jnp.int32, full, 0 if across else 1)
    return jnp.where(row == target, 1.0, 0.0).astype(BF16)


def column_of(row):
    return jnp.transpose(jnp.broadcast_to(row, (ROWS, ROWS)))


def body(
    hid, cnt, qry, ups, gain, wgt, lpn, lpo, adv, seg, trm,
    dq_out, dh_out, kg_out,
    hv, qv, uv, dqv, dhv, nb, dn, wbuf, wother, dbuf, ncols, acc, kvx, kvown, dkvown,
    pack_s, pack_r, unpack_s, unpack_r, pk, rv, pk2, rv2, inv, bias, coef, ps, rs, rd, og, kgv,
    local_sem, pair_send, pair_recv, w_send, w_recv, d_send, d_recv,
    n_send, n_recv, z_send, z_recv, b_send, b_recv, r_send, r_recv, o_send, o_recv,
):
    z = lax.axis_index("roll")
    f = lax.axis_index("fsdp")
    core = lax.rem(f, 2)
    other = 1 - core
    chip = f // 2
    x = lax.rem(chip, SIDE)
    y = chip // SIDE
    partner = chip * 2 + other

    barrier = pltpu.get_barrier_semaphore()
    pl.semaphore_signal(barrier, inc=1, device_id={"fsdp": partner}, device_id_type=MESH)
    for d in range(1, CHIPS):
        peer = lax.rem(chip + d, CHIPS) * 2 + core
        pl.semaphore_signal(barrier, inc=1, device_id={"fsdp": peer}, device_id_type=MESH)
    for d in range(1, ROLL):
        for who in (f, partner):
            pl.semaphore_signal(
                barrier, inc=1, device_id={"roll": lax.rem(z + d, ROLL), "fsdp": who}, device_id_type=MESH
            )

    def local(src, dst, n):
        copy = pltpu.make_async_copy(src, dst, local_sem.at[n])
        copy.start()
        return copy

    pair_copies = []

    def to_partner(src, dst, n):
        copy = pltpu.make_async_remote_copy(
            src_ref=src, dst_ref=dst, send_sem=pair_send.at[n], recv_sem=pair_recv.at[n],
            device_id={"fsdp": partner}, device_id_type=MESH,
        )
        copy.start()
        pair_copies.append(copy)

    def from_partner(dst, n):
        pltpu.make_async_copy(dst, dst, pair_recv.at[n]).wait()

    mine = pl.ds(pl.multiple_of(core * KVW, KVW), KVW)
    theirs = pl.ds(pl.multiple_of(other * KVW, KVW), KVW)
    w_copy = local(wgt.at[:, mine], wbuf.at[chip, core], 0)
    h_copy = local(hid, hv, 1)
    q_copy = local(qry, qv, 2)
    u_copy = local(ups, uv, 3)

    pl.semaphore_wait(barrier, 1 + (CHIPS - 1) + 2 * (ROLL - 1))

    to_partner(wgt.at[:, theirs], wbuf.at[chip, core], 0)
    w_copy.wait()
    gather = Gather(wbuf, w_send, w_recv, x, y, core)

    def by_owner(do):
        do(0)
        do(1)

    from_partner(wbuf.at[chip, other], 0)
    by_owner(gather.own)

    h_copy.wait()
    square = jnp.zeros((ROWS, HD), F32)
    for c in range(D // HD):
        part = hv[:, c * HD:(c + 1) * HD].astype(F32)
        square = square + part * part
    inv_rms = lax.rsqrt(jnp.sum(square, axis=1, keepdims=True) * (1.0 / D) + norm_eps)
    inv[...] = jnp.broadcast_to(inv_rms, (ROWS, HD))
    for c in range(CHIPS):
        cols = slice(c * CHIP_COLS, (c + 1) * CHIP_COLS)
        nb[core, :, cols] = (hv[:, cols].astype(F32) * inv_rms * gain[:, cols]).astype(BF16)
    to_partner(nb.at[core], nb.at[core], 1)

    gather.first_near(0)
    gather.first_near(1)

    n_copies = []
    for d in range(1, CHIPS):
        to = lax.rem(chip + d, CHIPS)
        copy = pltpu.make_async_remote_copy(
            src_ref=nb.at[core, :, pl.ds(pl.multiple_of(to * CHIP_COLS, CHIP_COLS), CHIP_COLS)],
            dst_ref=ncols.at[chip, core],
            send_sem=n_send.at[d], recv_sem=n_recv.at[d],
            device_id={"fsdp": to * 2 + core}, device_id_type=MESH,
        )
        n_copies.append(copy)

    send_counts = [cnt[0, z, l] for l in range(ROLL)]
    recv_counts = [cnt[0, s, z] for s in range(ROLL)]
    unpack_s[...] = selection(send_counts, True)
    unpack_r[...] = selection(recv_counts, True)
    pack_s[...] = selection(send_counts, False)
    pack_r[...] = selection(recv_counts, False)
    segment = seg[...]
    picked = jnp.zeros((1, ROWS), F32)
    for r in range(4):
        picked = picked + jnp.where(segment == r, adv[0, r], 0.0)
    weight = trm[...].astype(F32) * picked * jnp.minimum(jnp.exp(lpn[...] - lpo[...]), ratio_cap)
    coef[...] = column_of(weight)
    row = lax.broadcasted_iota(jnp.int32, (ROWS, ROWS), 0)
    col = lax.broadcasted_iota(jnp.int32, (ROWS, ROWS), 1)
    segment_f = segment.astype(F32)
    same = column_of(segment_f) == jnp.broadcast_to(segment_f, (ROWS, ROWS))
    bias[...] = jnp.where(same & (col <= row), 0.0, -jnp.inf)

    gather.second_near(0, 0)
    gather.second_near(1, 0)
    gather.first_far(0)
    gather.first_far(1)

    def project(c, first=False):
        cols = pl.ds(pl.multiple_of(c * CHIP_COLS, CHIP_COLS), CHIP_COLS)
        left = nb[:, :, cols].reshape(2 * ROWS, CHIP_COLS)
        term = dot(left, wbuf[c].reshape(2 * ROWS, KVW))
        if first:
            acc[...] = term
        else:
            acc[...] += term

    def chip_at(dx, dy):
        return lax.rem(y + dy + SIDE, SIDE) * SIDE + lax.rem(x + dx + SIDE, SIDE)

    from_partner(nb.at[other], 1)
    project(chip, True)
    for dx, dy in ((1, 0), (-1, 0), (0, 1), (0, -1)):
        project(chip_at(dx, dy))
    for j in (1, 2):
        gather.second_near(0, j)
        gather.second_near(1, j)
    for dx, dy in ((1, 1), (-1, 1), (1, -1), (-1, -1)):
        project(chip_at(dx, dy))
    gather.second_near(0, 3)
    gather.second_near(1, 3)
    gather.second_far(0, 0)
    gather.second_far(1, 0)
    for dx, dy in ((2, 0), (0, 2)):
        project(chip_at(dx, dy))
    for j in (1, 2):
        gather.second_far(0, j)
        gather.second_far(1, j)
    for dx, dy in ((2, 1), (2, -1), (1, 2), (-1, 2)):
        project(chip_at(dx, dy))
    gather.second_far(0, 3)
    gather.second_far(1, 3)
    project(chip_at(2, 2))

    for r in range(2):
        kvx[r] = acc[r * ROWS:(r + 1) * ROWS, :].astype(BF16)
    to_partner(kvx.at[other], kvown.at[core], 2)
    kvown[core] = kvx[core]
    from_partner(kvown.at[other], 2)

    def heads(ref, h):
        cols = slice(h * HD, (h + 1) * HD)
        return jnp.concatenate([ref[0, :, cols], ref[1, :, cols]], axis=0)

    z_copies = []

    def relay(out_buf, in_buf, send_sem, recv_sem, h):
        for d in range(1, ROLL):
            to = lax.rem(z + d, ROLL)
            copy = pltpu.make_async_remote_copy(
                src_ref=out_buf.at[h, to], dst_ref=in_buf.at[h, z],
                send_sem=send_sem.at[h, d], recv_sem=recv_sem.at[h, d],
                device_id={"roll": to}, device_id_type=MESH,
            )
            copy.start()
            z_copies.append(copy)
        in_buf[h, z] = out_buf[h, z]

    def relayed(in_buf, recv_sem, h):
        for d in range(1, ROLL):
            ref = in_buf.at[h, lax.rem(z + ROLL - d, ROLL)]
            pltpu.make_async_copy(ref, ref, recv_sem.at[h, d]).wait()

    for h in range(KV):
        packed = dot(pack_s[...], heads(kvown, h)).astype(BF16)
        pk[h] = packed.reshape(ROLL, 2 * SLOT, HD)
        relay(pk, rv, z_send, z_recv, h)

    to_partner(wbuf, wother, 3)
    for copy in n_copies:
        copy.start()
    n_own = local(
        nb.at[core, :, pl.ds(pl.multiple_of(chip * CHIP_COLS, CHIP_COLS), CHIP_COLS)],
        ncols.at[chip, core], 4,
    )
    q_copy.wait()
    u_copy.wait()
    scale = 1.0 / math.sqrt(HD)
    stacked = (GROUP, ROWS, ROWS)
    out_copies = []
    for h in range(KV):
        relayed(rv, z_recv, h)
        kv = dot(unpack_r[...], rv[h].reshape(PACKED, HD)).astype(BF16)
        keys, values = kv[:ROWS], kv[ROWS:]
        base = h * GROUP * HD
        q = jnp.concatenate([qv[:, base + g * HD:base + (g + 1) * HD] for g in range(GROUP)], axis=0)
        d_out = jnp.concatenate(
            [
                (coef[...] * uv[:, base + g * HD:base + (g + 1) * HD].astype(F32)).astype(BF16)
                for g in range(GROUP)
            ],
            axis=0,
        )
        scores = dot(q, keys, ((1,), (1,))).reshape(stacked) * scale + bias[...][None]
        d_probs = dot(d_out, values, ((1,), (1,))).reshape(stacked)
        expo = jnp.exp(scores - jnp.max(scores, axis=2, keepdims=True))
        probs = expo * (1.0 / jnp.sum(expo, axis=2, keepdims=True))
        probs_low = probs.astype(BF16)
        row_delta = jnp.sum(probs_low.astype(F32) * d_probs, axis=2, keepdims=True)
        d_scores = (probs * (d_probs - row_delta) * scale).astype(BF16)
        d_scores = d_scores.reshape(GROUP * ROWS, ROWS)
        probs_low = probs_low.reshape(GROUP * ROWS, ROWS)
        d_keys = dot(d_scores, q, ((0,), (0,)))
        d_values = dot(probs_low, d_out, ((0,), (0,)))
        d_rows = jnp.concatenate([d_keys, d_values], axis=0).astype(BF16)
        pk2[h] = dot(pack_r[...], d_rows).astype(BF16).reshape(ROLL, 2 * SLOT, HD)
        relay(pk2, rv2, b_send, b_recv, h)
        d_q = dot(d_scores, keys).astype(BF16)
        for g in range(GROUP):
            dqv[:, base + g * HD:base + (g + 1) * HD] = d_q[g * ROWS:(g + 1) * ROWS]
        out_copies.append(
            local(dqv.at[:, pl.ds(base, GROUP * HD)], dq_out.at[:, pl.ds(base, GROUP * HD)], 5 + h)
        )

    def span(g):
        return slice(g * WIDTH, (g + 1) * WIDTH)

    def returned(h):
        relayed(rv2, b_recv, h)
        back = dot(unpack_s[...], rv2[h].reshape(PACKED, HD)).astype(BF16)
        cols = slice(h * HD, (h + 1) * HD)
        dkvown[0, :, cols] = back[:ROWS]
        dkvown[1, :, cols] = back[ROWS:]

    def exchange(g):
        ds = pl.ds(g * WIDTH, WIDTH)
        to_partner(dkvown.at[other, :, ds], dbuf.at[chip, core, :, ds], 5 + g)
        dbuf[chip, core, :, span(g)] = dkvown[core, :, span(g)]

    backs = [
        Gather(dbuf, d_send.at[g], d_recv.at[g], x, y, core, span(g)) for g in range(D_CHUNKS)
    ]

    def begin(g):
        from_partner(dbuf.at[chip, other, :, pl.ds(g * WIDTH, WIDTH)], 5 + g)
        by_owner(backs[g].own)

    returned(0)
    returned(1)
    exchange(0)
    returned(2)
    begin(0)
    returned(3)
    exchange(1)
    for d in range(1, CHIPS):
        ref = ncols.at[lax.rem(chip + CHIPS - d, CHIPS), core]
        pltpu.make_async_copy(ref, ref, n_recv.at[d]).wait()
    n_own.wait()
    begin(1)
    to_partner(ncols.at[:, core], ncols.at[:, core], 4)
    from_partner(wother, 3)

    moment = [jnp.zeros((ROWS, HD), F32)]

    def row_grad(c):
        cols = slice(c * CHIP_COLS, (c + 1) * CHIP_COLS)
        d_n = dot(dkvown[core], wbuf[c].reshape(2 * ROWS, KVW), ((1,), (1,)))
        d_n = d_n + dot(dkvown[other], wother[c].reshape(2 * ROWS, KVW), ((1,), (1,)))
        d_n = d_n * gain[:, cols]
        dn[:, cols] = d_n
        for i in range(CHIP_COLS // HD):
            lanes = slice(c * CHIP_COLS + i * HD, c * CHIP_COLS + (i + 1) * HD)
            unit = hv[:, lanes].astype(F32) * inv[...]
            moment[0] = moment[0] + d_n[:, i * HD:(i + 1) * HD] * unit

    def row_out():
        mean = jnp.sum(moment[0], axis=1, keepdims=True) * (1.0 / D)
        inv_rms = inv[:, :1]
        for c in range(CHIPS):
            cols = slice(c * CHIP_COLS, (c + 1) * CHIP_COLS)
            unit = hv[:, cols].astype(F32) * inv_rms
            dhv[:, cols] = (inv_rms * (dn[:, cols] - unit * mean)).astype(BF16)
        out_copies.append(local(dhv, dh_out, 9))

    def grad(g, *offsets):
        cols = span(g)
        term = None
        for dx, dy in offsets:
            c = chip_at(dx, dy)
            left = ncols[c].reshape(2 * ROWS, CHIP_COLS)
            part = dot(left, dbuf[c, :, :, cols].reshape(2 * ROWS, WIDTH), ((0,), (0,)))
            term = part if term is None else term + part
        if (0, 0) in offsets:
            acc[:, cols] = term
        else:
            acc[:, cols] += term

    near = ((1, 0), (-1, 0), (0, 1), (0, -1))
    corners = ((1, 1), (-1, 1), (1, -1), (-1, -1))
    knights = ((2, 1), (2, -1), (1, 2), (-1, 2))

    def both(do, *args):
        do(0, *args)
        do(1, *args)

    grad_scale = 1.0 / math.sqrt(ROWS * 2 * CHIPS * ROLL)
    owner = z // (ROLL // 2)
    place = lax.rem(z, ROLL // 2)
    last = []

    def scatter(g):
        cols, ds = span(g), pl.ds(g * WIDTH, WIDTH)
        ps[:, :, cols] = (acc[:, cols] * grad_scale).astype(BF16).reshape(ROLL, SLICE, WIDTH)
        for d in range(1, ROLL):
            to = lax.rem(z + d, ROLL)
            copy = pltpu.make_async_remote_copy(
                src_ref=ps.at[to, :, ds], dst_ref=rs.at[z, :, ds],
                send_sem=r_send.at[g, d], recv_sem=r_recv.at[g, d],
                device_id={"roll": to}, device_id_type=MESH,
            )
            copy.start()
            last.append(copy)
        rs[z, :, cols] = ps[z, :, cols]

    def hand_over(to, d, g):
        ds = pl.ds(g * WIDTH, WIDTH)
        return pltpu.make_async_remote_copy(
            src_ref=rd.at[:, ds], dst_ref=og.at[core, place, :, ds],
            send_sem=o_send.at[g, d], recv_sem=o_recv.at[g, core, place],
            device_id={"roll": to, "fsdp": chip * 2 + owner}, device_id_type=MESH,
        )

    def reduce(g):
        cols, ds = span(g), pl.ds(g * WIDTH, WIDTH)
        for d in range(1, ROLL):
            ref = rs.at[lax.rem(z + ROLL - d, ROLL), :, ds]
            pltpu.make_async_copy(ref, ref, r_recv.at[g, d]).wait()
        total = rs[0, :, cols].astype(F32)
        for s in range(1, ROLL):
            total = total + rs[s, :, cols].astype(F32)
        rd[:, cols] = total.astype(BF16)
        for d in range(1, ROLL):
            copy = hand_over(lax.rem(z + d, ROLL), d, g)
            copy.start()
            last.append(copy)

        @pl.when(owner != core)
        def _():
            hand_over(z, 0, g).start()

        @pl.when(owner == core)
        def _():
            og[core, place, :, cols] = rd[:, cols]

    def collect(g):
        cols, ds = span(g), pl.ds(g * WIDTH, WIDTH)
        for s in range(ROLL // 2):
            for k in range(2):
                ref = og.at[k, s, :, ds]
                own = (core * (ROLL // 2) + s == z) & (core == k)

                @pl.when(jnp.logical_not(own))
                def _():
                    pltpu.make_async_copy(ref, ref, o_recv.at[g, k, s]).wait()

        for k in range(2):
            out = slice(k * KVW + cols.start, k * KVW + cols.stop)
            kgv[:, out] = og[k, :, :, cols].astype(F32).reshape(ROWS, WIDTH)

    first, second = backs
    both(first.first_near)
    for c in range(0, 3):
        row_grad(c)
    both(first.second_near, 0)
    both(first.first_far)
    both(second.first_near)
    for c in range(3, 6):
        row_grad(c)
    both(first.second_near, 1)
    both(first.second_near, 2)
    both(second.second_near, 0)
    both(second.first_far)
    from_partner(ncols.at[:, other], 4)
    grad(0, (0, 0), *near)
    both(first.second_near, 3)
    both(second.second_near, 1)
    both(second.second_near, 2)
    grad(0, *corners)
    both(first.second_far, 0)
    grad(0, (2, 0), (0, 2))
    both(first.second_far, 1)
    both(first.second_far, 2)
    grad(0, *knights)
    both(first.second_far, 3)
    grad(0, (2, 2))
    scatter(0)
    both(second.second_near, 3)
    for c in range(6, 16):
        row_grad(c)
    grad(1, (0, 0), *near, *corners)
    row_out()
    both(second.second_far, 0)
    grad(1, (2, 0), (0, 2))
    both(second.second_far, 1)
    both(second.second_far, 2)
    grad(1, *knights)
    both(second.second_far, 3)
    grad(1, (2, 2))
    scatter(1)
    reduce(0)
    reduce(1)
    collect(0)
    collect(1)
    out_copies.append(local(kgv, kg_out, 10))

    @pl.when(owner != core)
    def _():
        for g in range(D_CHUNKS):
            hand_over(z, 0, g).wait_send()

    gather.finish()
    for back in backs:
        back.finish()
    for copy in pair_copies + n_copies + z_copies + last:
        copy.wait_send()
    for copy in out_copies:
        copy.wait()


def store(*refs):
    sources, outs, buffers, (in_sem, out_sem) = refs[:3], refs[3:6], refs[6:9], refs[9:]
    arrivals, leaving = [], []
    rows = ROWS // PIECES
    for piece in range(PIECES):
        part = pl.ds(piece * rows, rows)
        for n in range(3):
            copy = pltpu.make_async_copy(sources[n].at[part], buffers[n].at[part], in_sem.at[n, piece])
            copy.start()
            arrivals.append((copy, n, piece, part))
    for copy, n, piece, part in arrivals:
        copy.wait()
        out = pltpu.make_async_copy(buffers[n].at[part], outs[n].at[part], out_sem.at[n, piece])
        out.start()
        leaving.append(out)
    for out in leaving:
        out.wait()


def shards(
    hidden, send_counts, queries, upstream, norm_gain, kv_weight,
    logp_new, logp_old, advantage, segment_ids, trim_mask,
):
    anywhere = pl.BlockSpec(memory_space=pl.ANY)
    vmem = pl.BlockSpec(memory_space=pltpu.VMEM)
    smem = pl.BlockSpec(memory_space=pltpu.SMEM)
    dma = pltpu.SemaphoreType.DMA
    relay_buf = pltpu.VMEM((KV, ROLL, 2 * SLOT, HD), BF16)
    rows = pltpu.VMEM((ROWS, D), BF16)
    results = pl.pallas_call(
        body,
        out_shape=(
            jax.ShapeDtypeStruct((ROWS, D), BF16),
            jax.ShapeDtypeStruct((ROWS, D), BF16),
            jax.ShapeDtypeStruct((ROWS, 2 * KVW), F32),
        ),
        in_specs=[anywhere, smem, anywhere, anywhere, vmem, anywhere, vmem, vmem, smem, vmem, vmem],
        out_specs=(anywhere, anywhere, anywhere),
        scratch_shapes=[
            rows, rows, rows, rows, rows,
            pltpu.VMEM((2, ROWS, D), BF16),
            pltpu.VMEM((ROWS, D), F32),
            pltpu.VMEM((CHIPS, 2, ROWS, KVW), BF16),
            pltpu.VMEM((CHIPS, 2, ROWS, KVW), BF16),
            pltpu.VMEM((CHIPS, 2, ROWS, KVW), BF16),
            pltpu.VMEM((CHIPS, 2, ROWS, CHIP_COLS), BF16),
            pltpu.VMEM((2 * ROWS, KVW), F32),
            pltpu.VMEM((2, ROWS, KVW), BF16),
            pltpu.VMEM((2, ROWS, KVW), BF16),
            pltpu.VMEM((2, ROWS, KVW), BF16),
            pltpu.VMEM((PACKED, 2 * ROWS), BF16),
            pltpu.VMEM((PACKED, 2 * ROWS), BF16),
            pltpu.VMEM((2 * ROWS, PACKED), BF16),
            pltpu.VMEM((2 * ROWS, PACKED), BF16),
            relay_buf, relay_buf, relay_buf, relay_buf,
            pltpu.VMEM((ROWS, HD), F32),
            pltpu.VMEM((ROWS, ROWS), F32),
            pltpu.VMEM((ROWS, ROWS), F32),
            pltpu.VMEM((ROLL, SLICE, KVW), BF16),
            pltpu.VMEM((ROLL, SLICE, KVW), BF16),
            pltpu.VMEM((SLICE, KVW), BF16),
            pltpu.VMEM((2, ROLL // 2, SLICE, KVW), BF16),
            pltpu.VMEM((ROWS, 2 * KVW), F32),
            dma((11,)), dma((7,)), dma((7,)),
            dma((40,)), dma((2, 20)), dma((D_CHUNKS, 40)), dma((D_CHUNKS, 2, 20)),
            dma((CHIPS,)), dma((CHIPS,)),
            dma((KV, ROLL)), dma((KV, ROLL)), dma((KV, ROLL)), dma((KV, ROLL)),
            dma((D_CHUNKS, ROLL)), dma((D_CHUNKS, ROLL)), dma((D_CHUNKS, ROLL)), dma((D_CHUNKS, 2, ROLL // 2)),
        ],
        compiler_params=pltpu.CompilerParams(
            collective_id=0, has_side_effects=True, vmem_limit_bytes=60 << 20
        ),
        name="backward",
    )(
        hidden, send_counts, queries, upstream, norm_gain.reshape(1, D), kv_weight,
        logp_new, logp_old, advantage, segment_ids, trim_mask,
    )
    return pl.pallas_call(
        store,
        out_shape=tuple(jax.ShapeDtypeStruct(a.shape, a.dtype) for a in results),
        in_specs=[anywhere] * 3,
        out_specs=(anywhere,) * 3,
        scratch_shapes=[pltpu.VMEM(a.shape, a.dtype) for a in results] + [dma((3, PIECES)), dma((3, PIECES))],
        compiler_params=pltpu.CompilerParams(vmem_limit_bytes=60 << 20),
        name="store",
    )(*results)


def solution(mesh):
    placed = (
        P(("roll", "fsdp"), None),
        P("fsdp", None, None),
        P(("roll", "fsdp"), None),
        P(("roll", "fsdp"), None),
        P(),
        P("fsdp", None),
        P(("roll", "fsdp"), None),
        P(("roll", "fsdp"), None),
        P(("roll", "fsdp"), None),
        P(("roll", "fsdp"), None),
        P(("roll", "fsdp"), None),
    )
    return jax.shard_map(
        shards,
        mesh=mesh,
        in_specs=placed,
        out_specs=(P(("roll", "fsdp"), None), P(("roll", "fsdp"), None), P("fsdp", None)),
        check_vma=False,
    )
```
